32 devices in a mesh: tok: 8 (over z, y), head: 4 (over x, core).
Axes of the slice: x: 2, y: 2, z: 4, core: 2. Of those that a mesh axis runs over, the one named last changes fastest.
Arguments:
- tokens: bfloat16 [2, 12288, 768], P(None, ('tok', 'head')), may hold values from -6 to 6
- crop_start: int32 [2, 8, 29], P(None, 'tok'), may hold values from 0 to 1536, as said below
- crop_len: int32 [2, 8, 29], P(None, 'tok'), may hold values from 0 to 261, as said below
- attn_gain: float32 [768], replicated, may hold values from 0.5 to 1.5
- attn_shift: float32 [768], replicated, may hold values from -1.2 to 1.2
- qkv_weight: bfloat16 [768, 2304], replicated, may hold values from -0.21875 to 0.21875
- query_bias: float32 [768], replicated, may hold values from -1.2 to 1.2
- value_bias: float32 [768], replicated, may hold values from -1.2 to 1.2
- out_weight: bfloat16 [768, 768], replicated, may hold values from -0.625 to 0.625
- out_bias: float32 [768], replicated, may hold values from -1.2 to 1.2
- attn_scale: float32 [768], replicated, may hold values from 0.5 to 2
- mlp_gain: float32 [768], replicated, may hold values from 0.5 to 1.5
- mlp_shift: float32 [768], replicated, may hold values from -1.2 to 1.2
- up_weight: bfloat16 [768, 3072], replicated, may hold values from -0.21875 to 0.21875
- up_bias: float32 [3072], replicated, may hold values from -1.2 to 1.2
- down_weight: bfloat16 [3072, 768], replicated, may hold values from -0.109375 to 0.109375
- down_bias: float32 [768], replicated, may hold values from -1.2 to 1.2
- mlp_scale: float32 [768], replicated, may hold values from 0.5 to 2
- cotangent: bfloat16 [2, 12288, 768], P(None, ('tok', 'head')), may hold values from -6 to 6
Outputs:
- output: bfloat16 [2, 12288, 768], P(None, ('tok', 'head'))
- input_grad: float32 [2, 12288, 768], P(None, ('tok', 'head'))
- grad_attn_gain: float32 [768], replicated
- grad_attn_shift: float32 [768], replicated
- grad_qkv_weight: float32 [768, 2304], P('head', 'tok')
- grad_query_bias: float32 [768], replicated
- grad_value_bias: float32 [768], replicated
- grad_out_weight: float32 [768, 768], P('head', 'tok')
- grad_out_bias: float32 [768], replicated
- grad_attn_scale: float32 [768], replicated
- grad_mlp_gain: float32 [768], replicated
- grad_mlp_shift: float32 [768], replicated
- grad_up_weight: float32 [768, 3072], P('head', 'tok')
- grad_up_bias: float32 [3072], replicated
- grad_down_weight: float32 [3072, 768], P('head', 'tok')
- grad_down_bias: float32 [768], replicated
- grad_mlp_scale: float32 [768], replicated
The draws below stay inside these ranges and needn't reach their ends.
Inputs may be any that keep to these rules, and one draw needn't show every extreme that they name: `crop_start`: used slots come first in every group and lie end to end from row 0; an unused slot starts at 1536. `crop_len`: used slots hold 261 or 54 rows, slot 0 always 261; unused slots hold 0.
All inputs are finite; a program needn't handle non-finite values.
Results may differ from the reference program's by a relative error of at most 0.013.
Values may be sent and summed in bfloat16 or wider, within the bound.
No kernel may reach another device: no remote copies, remote signals or barrier semaphores. Data moves between devices by JAX's collectives and lax.ppermute only.
A program may use at most 256 MiB of HBM per device.

```python
import math
import jax
import jax.numpy as jnp
from jax import lax

D = 768
HEADS = 12
HEAD_DIM = 64
FF = 3072
MICRO = 2
GLOBAL_LEN = 261
LOCAL_LEN = 54
GROUP = 1536
GROUPS = 8
TOKENS = 12288
CROPS = 29


def crop_table(key):
    base_key = jax.random.fold_in(key, 7)
    kind_key, limit_key = jax.random.split(base_key)
    kind_draw = jax.random.randint(kind_key, (MICRO, GROUPS, CROPS), 0, 10)
    is_global = (kind_draw < 3).at[:, :, 0].set(True)
    lengths = jnp.where(is_global, GLOBAL_LEN, LOCAL_LEN).astype(jnp.int32)
    slot_ends = jnp.cumsum(lengths, axis=-1).astype(jnp.int32)
    capacity = GROUP - jax.random.randint(limit_key, (MICRO, GROUPS, 1), 0, GROUP // 2)
    in_use = slot_ends <= capacity
    starts = jnp.where(in_use, slot_ends - lengths, GROUP).astype(jnp.int32)
    return (starts, jnp.where(in_use, lengths, 0).astype(jnp.int32))


def draw_crop_start(key, part):
    return crop_table(key)[0]


def draw_crop_len(key, part):
    return crop_table(key)[1]


def spiked(drawn, rng, source, target, parts, factor):
    def block_of(dim):
        return (jnp.arange(drawn.shape[dim]) // (drawn.shape[dim] // parts)).reshape((-1,) + (1,) * (drawn.ndim - 1 - dim))

    one_side = jax.random.permutation(rng, parts)[block_of(target)]
    second = (block_of(target) + parts // 2) % parts
    return jnp.where((block_of(source) == one_side) | (block_of(source) == second), factor * drawn, drawn)


def levels(stream_key, extent, cuts, least, largest):
    level, own = 1.0, jax.random.fold_in(stream_key, 6)
    for dim, blocks in cuts:
        heights = jnp.exp(jax.random.uniform(jax.random.fold_in(own, dim), (blocks,), jnp.float32, least / len(cuts), largest / len(cuts)))
        level = level * jnp.repeat(heights, extent[dim] // blocks).reshape([-1 if axis == dim else 1 for axis in range(len(extent))])
    return level


def normal_values(stream_key, shape, deviation, limit, cuts=(), kind=jnp.bfloat16):
    values = deviation * jax.random.normal(stream_key, shape, jnp.float32)
    if cuts:
        values = values * levels(stream_key, shape, cuts, -0.22, 0.18)
    return jnp.clip(values, -limit, limit).astype(kind)


def gaussian_with(rng, shape, width, most, shards, heavy, kind=jnp.bfloat16):
    drawn = width * jax.random.normal(rng, shape, jnp.float32)
    if shards:
        drawn = drawn * levels(rng, shape, shards, -0.22, 0.18)
    return jnp.clip(spiked(drawn, jax.random.fold_in(rng, 3), *heavy), -most, most).astype(kind)


def setup_inputs(seed: int = 0) -> dict:
    seeds = jax.random.split(jax.random.key(seed), 20)
    tokens = normal_values(seeds[0], (MICRO, TOKENS, D), 1.0, 6.0, ((1, 32),))
    crop_start = draw_crop_start(jax.random.fold_in(seeds[19], 71), 0)
    crop_len = draw_crop_len(jax.random.fold_in(seeds[19], 71), 0)
    attn_gain = jnp.clip(1.0 + 0.1 * jax.random.normal(seeds[3], (D,), jnp.float32), 0.5, 1.5)
    attn_shift = normal_values(seeds[4], (D,), 0.3, 1.2, (), jnp.float32)
    qkv_weight = normal_values(seeds[5], (D, 3 * D), D ** -0.5, 0.21875)
    query_bias = normal_values(seeds[6], (D,), 0.3, 1.2, (), jnp.float32)
    value_bias = normal_values(seeds[7], (D,), 0.3, 1.2, (), jnp.float32)
    out_weight = normal_values(seeds[8], (D, D), (D // 8) ** -0.5, 0.625)
    out_bias = normal_values(seeds[9], (D,), 0.3, 1.2, (), jnp.float32)
    attn_scale = jnp.clip(jnp.exp(jax.random.uniform(seeds[10], (D,), jnp.float32, math.log(0.5), math.log(2.0))), 0.5, 2.0)
    mlp_gain = jnp.clip(1.0 + 0.1 * jax.random.normal(seeds[11], (D,), jnp.float32), 0.5, 1.5)
    mlp_shift = normal_values(seeds[12], (D,), 0.3, 1.2, (), jnp.float32)
    up_weight = normal_values(seeds[13], (D, FF), D ** -0.5, 0.21875)
    up_bias = normal_values(seeds[14], (FF,), 0.3, 1.2, (), jnp.float32)
    down_weight = normal_values(seeds[15], (FF, D), FF ** -0.5, 0.109375)
    down_bias = normal_values(seeds[16], (D,), 0.3, 1.2, (), jnp.float32)
    mlp_scale = jnp.clip(jnp.exp(jax.random.uniform(seeds[17], (D,), jnp.float32, math.log(0.5), math.log(2.0))), 0.5, 2.0)
    cotangent = gaussian_with(seeds[18], (MICRO, TOKENS, D), 1.0, 6.0, ((1, 32),), (1, 2, 32, 2.75))
    return dict(tokens=tokens, crop_start=crop_start, crop_len=crop_len, attn_gain=attn_gain, attn_shift=attn_shift, qkv_weight=qkv_weight, query_bias=query_bias, value_bias=value_bias, out_weight=out_weight, out_bias=out_bias, attn_scale=attn_scale, mlp_gain=mlp_gain, mlp_shift=mlp_shift, up_weight=up_weight, up_bias=up_bias, down_weight=down_weight, down_bias=down_bias, mlp_scale=mlp_scale, cotangent=cotangent)


NORM_EPS = 1e-06
MASKED = -1e+30
PRECISE = lax.Precision.HIGHEST

@jax.custom_vjp
def low(v):
    return lax.optimization_barrier(v.astype(jnp.bfloat16)).astype(jnp.float32)

@jax.custom_vjp
def low_back(v):
    return v

def low_keep(v):
    return (low(v), None)

def low_pass(kept, grad):
    return (grad,)

def back_keep(v):
    return (v, None)

def back_low(kept, grad):
    return (low(grad),)
low.defvjp(low_keep, low_pass)
low_back.defvjp(back_keep, back_low)

def layer_norm(values, gain, shift):
    center = lax.optimization_barrier(jnp.mean(values, axis=-1, keepdims=True))
    centered = values - center
    variance = lax.optimization_barrier(jnp.mean(centered * centered, axis=-1, keepdims=True))
    return centered * lax.rsqrt(variance + NORM_EPS) * gain + shift

def segment_ids(starts, lengths):
    row_ids = jnp.arange(GROUP, dtype=jnp.int32)[:, None]
    inside = (row_ids >= starts[None, :]) & (row_ids < (starts + lengths)[None, :])
    slot_ids = jnp.arange(CROPS, dtype=jnp.int32)[None, :]
    found = lax.optimization_barrier(jnp.sum(jnp.where(inside, slot_ids, 0), axis=1)).astype(jnp.int32)
    return jnp.where(jnp.any(inside, axis=1), found, -1 - row_ids[:, 0]).astype(jnp.int32)

def attend_group(inputs):
    queries, key_rows, value_rows, segment = inputs
    scores = jnp.einsum('qhd,khd->hqk', queries, key_rows, precision=PRECISE) * HEAD_DIM ** (-0.5)
    scores = low_back(scores)
    same = segment[:, None] == segment[None, :]
    scores = jnp.where(same[None], scores, MASKED)
    row_max = lax.optimization_barrier(jnp.max(scores, axis=-1, keepdims=True))
    exponent = jnp.exp(scores - row_max)
    attn_probs = low(exponent / lax.optimization_barrier(jnp.sum(exponent, axis=-1, keepdims=True)))
    return jnp.einsum('hqk,khd->qhd', attn_probs, value_rows, precision=PRECISE)

def forward(tokens, attn_gain, attn_shift, qkv_weight, query_bias, value_bias, out_weight, out_bias, attn_scale, mlp_gain, mlp_shift, up_weight, up_bias, down_weight, down_bias, mlp_scale, segments):
    attn_normed = low(layer_norm(tokens, attn_gain, attn_shift))
    projected = jnp.einsum('mtd,de->mte', attn_normed, qkv_weight, precision=PRECISE)
    queries = low(low_back(projected[..., :D] + query_bias))
    key_rows = low(low_back(projected[..., D:2 * D]))
    value_rows = low(low_back(projected[..., 2 * D:] + value_bias))
    shape = (MICRO * GROUPS, GROUP, HEADS, HEAD_DIM)
    attended = lax.map(jax.checkpoint(attend_group), (queries.reshape(shape), key_rows.reshape(shape), value_rows.reshape(shape), segments))
    attended = low(low_back(attended.reshape(MICRO, TOKENS, D)))
    attn_branch = low_back(jnp.einsum('mtd,de->mte', attended, out_weight, precision=PRECISE) + out_bias)
    mid = tokens + attn_scale * attn_branch
    mlp_normed = low(layer_norm(mid, mlp_gain, mlp_shift))
    up_pre = low_back(jnp.einsum('mtd,df->mtf', mlp_normed, up_weight, precision=PRECISE) + up_bias)
    activated = low(jax.nn.gelu(up_pre, approximate=False))
    mlp_branch = low_back(jnp.einsum('mtf,fd->mtd', activated, down_weight, precision=PRECISE) + down_bias)
    return mid + mlp_scale * mlp_branch

def reference(tokens, crop_start, crop_len, attn_gain, attn_shift, qkv_weight, query_bias, value_bias, out_weight, out_bias, attn_scale, mlp_gain, mlp_shift, up_weight, up_bias, down_weight, down_bias, mlp_scale, cotangent):
    starts = crop_start.reshape(MICRO * GROUPS, CROPS).astype(jnp.int32)
    lengths = crop_len.reshape(MICRO * GROUPS, CROPS).astype(jnp.int32)
    segments = jax.vmap(segment_ids)(starts, lengths)

    def run(*values):
        return forward(*values, segments)
    result, pullback = jax.vjp(run, tokens.astype(jnp.float32), attn_gain, attn_shift, qkv_weight.astype(jnp.float32), query_bias, value_bias, out_weight.astype(jnp.float32), out_bias, attn_scale, mlp_gain, mlp_shift, up_weight.astype(jnp.float32), up_bias, down_weight.astype(jnp.float32), down_bias, mlp_scale)
    grads = pullback(cotangent.astype(jnp.float32))
    return (result.astype(jnp.bfloat16), grads[0], grads[1], grads[2], grads[3], grads[4], grads[5], grads[6], grads[7], grads[8], grads[9], grads[10], grads[11], grads[12], grads[13], grads[14], grads[15])
```

```python
from functools import partial

import jax
import jax.numpy as jnp
from jax import lax
from jax.experimental import pallas as pl
from jax.experimental.pallas import tpu as pltpu
from jax.sharding import PartitionSpec as P

HEAD_DIM = 64
NORM_EPS = 1e-06
MASKED = -1e30
HALO = 272
QT = 128
LANES = 128
F32 = jnp.float32
BF16 = jnp.bfloat16


def norm_stats(values):
    center = jnp.mean(values, axis=-1, keepdims=True)
    centered = values - center
    variance = jnp.mean(centered * centered, axis=-1, keepdims=True)
    inv_std = lax.rsqrt(variance + NORM_EPS)
    return centered * inv_std, inv_std


def norm_backward(grad_out, gain, normal_rows, inv_std):
    scaled = grad_out * gain
    mean_one = jnp.mean(scaled, axis=-1, keepdims=True)
    mean_two = jnp.mean(scaled * normal_rows, axis=-1, keepdims=True)
    grad_in = inv_std * (scaled - mean_one - normal_rows * mean_two)
    return grad_in, jnp.sum(grad_out * normal_rows, axis=0), jnp.sum(grad_out, axis=0)


def dot_nn(a, b):
    return lax.dot_general(a, b, (((1,), (0,)), ((), ())), preferred_element_type=F32)


def dot_nt(a, b):
    return lax.dot_general(a, b, (((1,), (1,)), ((), ())), preferred_element_type=F32)


def dot_tn(a, b):
    return lax.dot_general(a, b, (((0,), (0,)), ((), ())), preferred_element_type=F32)


def crop_bounds(starts, lengths, first_row, rows, group_rows):
    row_ids = first_row + lax.iota(jnp.int32, rows)[:, None]
    ends = jnp.minimum(starts + lengths, group_rows)
    inside = (row_ids >= starts[None, :]) & (row_ids < ends[None, :])
    found = jnp.any(inside, axis=1)
    low = jnp.where(found, jnp.sum(jnp.where(inside, starts[None, :], 0), axis=1), row_ids[:, 0])
    high = jnp.where(found, jnp.sum(jnp.where(inside, ends[None, :], 0), axis=1), row_ids[:, 0] + 1)
    return low - first_row + HALO, high - first_row + HALO


def tile_ranges(low, high, window):
    tiles = low.shape[0] // QT
    first = (low.reshape(tiles, QT)[:, 0] // 16) * 16
    last = high.reshape(tiles, QT)[:, QT - 1]
    count = jnp.clip((last - first + LANES - 1) // LANES, 1, 6)
    first = jnp.clip(first, 0, window - count * LANES)
    return jnp.concatenate([first, count]).astype(jnp.int32)


def load_window(left, own, right, win, width):
    rows = own.shape[0]
    win[0:HALO, :] = left[...]
    win[HALO : HALO + rows, :] = own[:, width:]
    win[HALO + rows :, :] = right[...]


def pair_stack(values):
    lane = lax.broadcasted_iota(jnp.int32, values.shape, 1)
    zero = jnp.zeros_like(values)
    one = jnp.where(lane < HEAD_DIM, values, zero)
    two = jnp.where(lane < HEAD_DIM, zero, values)
    return jnp.concatenate([one, two], axis=0)


def pair_merge(values):
    half = values.shape[0] // 2
    lane = lax.broadcasted_iota(jnp.int32, (half, LANES), 1)
    return jnp.where(lane < HEAD_DIM, values[:half], values[half:])


def tile_bias(low_ref, high_ref, row0, first, span):
    cols = first + lax.broadcasted_iota(jnp.int32, (QT, span), 1)
    low = low_ref[pl.ds(row0, QT), :]
    high = high_ref[pl.ds(row0, QT), :]
    same = (cols >= low) & (cols < high)
    bias = jnp.where(same, 0.0, MASKED).astype(F32)
    return jnp.concatenate([bias, bias], axis=0)


def forward_kernel(ranges, low_ref, high_ref, left, own, right, out, win):
    width = out.shape[1]
    rows = own.shape[0]
    tiles = rows // QT
    load_window(left, own, right, win, width)

    def tile(i, carry):
        row0 = pl.multiple_of(i * QT, QT)
        first = pl.multiple_of(ranges[i], 16)
        count = ranges[tiles + i]
        for n in range(1, 7):

            @pl.when(count == n)
            def _():
                span = n * LANES
                bias = tile_bias(low_ref, high_ref, row0, first, span)

                def pair(p, inner):
                    col = pl.multiple_of(p * LANES, LANES)
                    vcol = pl.multiple_of(width + p * LANES, LANES)
                    query = own[pl.ds(row0, QT), pl.ds(col, LANES)]
                    stacked = pair_stack(query * jnp.asarray(0.125, BF16))
                    keys = win[pl.ds(first, span), pl.ds(col, LANES)]
                    scores = dot_nt(stacked, keys) + bias
                    peak = jnp.max(scores, axis=1, keepdims=True)
                    expo = jnp.exp(scores - peak)
                    total = jnp.sum(expo, axis=1, keepdims=True)
                    vals = win[pl.ds(first, span), pl.ds(vcol, LANES)]
                    res = dot_nn(expo.astype(BF16), vals) / total
                    out[pl.ds(row0, QT), pl.ds(col, LANES)] = pair_merge(res).astype(BF16)
                    return inner

                lax.fori_loop(0, width // LANES, pair, 0)

        return carry

    lax.fori_loop(0, tiles, tile, 0)


def backward_kernel(
    ranges, low_ref, high_ref, left, own, right, grad, dq, dleft, down, dright, win, acc
):
    width = grad.shape[1]
    rows = own.shape[0]
    tiles = rows // QT
    load_window(left, own, right, win, width)
    acc[...] = jnp.zeros_like(acc)

    def tile(i, carry):
        row0 = pl.multiple_of(i * QT, QT)
        first = pl.multiple_of(ranges[i], 16)
        count = ranges[tiles + i]
        for n in range(1, 7):

            @pl.when(count == n)
            def _():
                span = n * LANES
                bias = tile_bias(low_ref, high_ref, row0, first, span)

                def pair(p, inner):
                    col = pl.multiple_of(p * LANES, LANES)
                    vcol = pl.multiple_of(width + p * LANES, LANES)
                    query = own[pl.ds(row0, QT), pl.ds(col, LANES)]
                    stacked = pair_stack(query * jnp.asarray(0.125, BF16))
                    gstack = pair_stack(grad[pl.ds(row0, QT), pl.ds(col, LANES)])
                    keys = win[pl.ds(first, span), pl.ds(col, LANES)]
                    vals = win[pl.ds(first, span), pl.ds(vcol, LANES)]
                    scores = dot_nt(stacked, keys) + bias
                    peak = jnp.max(scores, axis=1, keepdims=True)
                    expo = jnp.exp(scores - peak)
                    total = jnp.sum(expo, axis=1, keepdims=True)
                    probs = expo * (1.0 / total)
                    dprobs = dot_nt(gstack, vals)
                    row_dot = jnp.sum(probs * dprobs, axis=1, keepdims=True)
                    dscores = (probs * (dprobs - row_dot)).astype(BF16)
                    res = dot_nn(dscores, keys) * 0.125
                    dq[pl.ds(row0, QT), pl.ds(col, LANES)] = pair_merge(res).astype(BF16)
                    acc[pl.ds(first, span), pl.ds(col, LANES)] += dot_tn(dscores, stacked)
                    acc[pl.ds(first, span), pl.ds(vcol, LANES)] += dot_tn(
                        probs.astype(BF16), gstack
                    )
                    return inner

                lax.fori_loop(0, width // LANES, pair, 0)

        return carry

    lax.fori_loop(0, tiles, tile, 0)
    dleft[...] = acc[0:HALO, :].astype(BF16)
    down[...] = acc[HALO : HALO + rows, :]
    dright[...] = acc[HALO + rows :, :].astype(BF16)


def smem():
    return pl.BlockSpec(memory_space=pltpu.SMEM)


def vmem():
    return pl.BlockSpec(memory_space=pltpu.VMEM)


def attention_forward(ranges, low, high, left, own, right):
    rows, width = own.shape[0], own.shape[1] // 3
    window = rows + 2 * HALO
    return pl.pallas_call(
        forward_kernel,
        out_shape=jax.ShapeDtypeStruct((rows, width), BF16),
        in_specs=[smem()] + [vmem()] * 5,
        out_specs=vmem(),
        scratch_shapes=[pltpu.VMEM((window, 2 * width), BF16)],
        cost_estimate=pl.CostEstimate(
            flops=4 * rows * 640 * width * 4, bytes_accessed=8 * 1024 * 1024, transcendentals=0
        ),
        name="attn_fwd",
    )(ranges, low, high, left, own, right)


def attention_backward(ranges, low, high, left, own, right, grad):
    rows, width = grad.shape
    window = rows + 2 * HALO
    return pl.pallas_call(
        backward_kernel,
        out_shape=(
            jax.ShapeDtypeStruct((rows, width), BF16),
            jax.ShapeDtypeStruct((HALO, 2 * width), BF16),
            jax.ShapeDtypeStruct((rows, 2 * width), F32),
            jax.ShapeDtypeStruct((HALO, 2 * width), BF16),
        ),
        in_specs=[smem()] + [vmem()] * 6,
        out_specs=(vmem(),) * 4,
        scratch_shapes=[
            pltpu.VMEM((window, 2 * width), BF16),
            pltpu.VMEM((window, 2 * width), F32),
        ],
        cost_estimate=pl.CostEstimate(
            flops=10 * rows * 640 * width * 4, bytes_accessed=16 * 1024 * 1024, transcendentals=0
        ),
        name="attn_bwd",
    )(ranges, low, high, left, own, right, grad)


def shift_right(values, size):
    return lax.ppermute(values, "head", [(i, i + 1) for i in range(size - 1)])


def shift_left(values, size):
    return lax.ppermute(values, "head", [(i + 1, i) for i in range(size - 1)])


def axis_bits(size):
    return size.bit_length() - 1


def bit_orders(tok_size, head_size):
    tok = [("tok", b) for b in range(axis_bits(tok_size))]
    head = [("head", b) for b in range(axis_bits(head_size))]
    return head + tok, head[:1] + tok + head[1:]


def swap_pairs(size, bit):
    return [(i, i ^ (1 << bit)) for i in range(size)]


def reduce_blocks(blocks, order, sizes):
    dims = [("tok", b) for b in reversed(range(axis_bits(sizes["tok"])))]
    dims += [("head", b) for b in reversed(range(axis_bits(sizes["head"])))]
    part = blocks.reshape((2,) * len(dims) + blocks.shape[2:])
    for step, (axis, bit) in enumerate(order):
        where = dims.index((axis, bit))
        mine = (lax.axis_index(axis) >> bit) & 1
        send = lax.dynamic_index_in_dim(part, 1 - mine, where, keepdims=False)
        keep = lax.dynamic_index_in_dim(part, mine, where, keepdims=False)
        got = lax.ppermute(send, axis, swap_pairs(sizes[axis], bit))
        part = keep.astype(F32) + got.astype(F32)
        if step + 1 < len(order):
            part = part.astype(BF16)
        dims.pop(where)
    return part


def reduce_small(values, order, sizes):
    for axis, bit in order:
        values = values + lax.ppermute(values, axis, swap_pairs(sizes[axis], bit))
    return values


def per_device(
    sizes,
    tokens,
    crop_start,
    crop_len,
    attn_gain,
    attn_shift,
    qkv_weight,
    query_bias,
    value_bias,
    out_weight,
    out_bias,
    attn_scale,
    mlp_gain,
    mlp_shift,
    up_weight,
    up_bias,
    down_weight,
    down_bias,
    mlp_scale,
    cotangent,
):
    micro, rows, width = tokens.shape
    hidden = up_weight.shape[1]
    tok_size, head_size = sizes["tok"], sizes["head"]
    window = rows + 2 * HALO
    head_at = lax.axis_index("head")
    order_a, order_b = bit_orders(tok_size, head_size)
    kv_bias = jnp.concatenate([jnp.zeros_like(value_bias), value_bias])
    qkv_bias = jnp.concatenate([query_bias, kv_bias])

    halo_left = shift_right(tokens[:, rows - HALO :, :], head_size)
    halo_right = shift_left(tokens[:, :HALO, :], head_size)

    total_rows = micro * rows
    inputs_f = tokens.reshape(total_rows, width).astype(F32)
    normal_one, inv_one = norm_stats(inputs_f)
    normed_low = (normal_one * attn_gain + attn_shift).astype(BF16)
    qkv = (dot_nn(normed_low, qkv_weight) + qkv_bias).astype(BF16)

    halo = jnp.stack([halo_left, halo_right]).reshape(2 * micro * HALO, width)
    halo_normal, _ = norm_stats(halo.astype(F32))
    halo_low = (halo_normal * attn_gain + attn_shift).astype(BF16)
    halo_kv = (dot_nn(halo_low, qkv_weight[:, width:]) + kv_bias).astype(BF16)
    halo_kv = halo_kv.reshape(2, micro, HALO, 2 * width)

    bounds = []
    attended_parts = []
    for m in range(micro):
        low, high = crop_bounds(
            crop_start[m, 0], crop_len[m, 0], head_at * rows, rows, head_size * rows
        )
        ranges = tile_ranges(low, high, window)
        bounds.append((ranges, low[:, None], high[:, None]))
        own = qkv[m * rows : (m + 1) * rows]
        attended_parts.append(attention_forward(*bounds[m], halo_kv[0, m], own, halo_kv[1, m]))
    attended = jnp.concatenate(attended_parts, axis=0)

    attn_branch = dot_nn(attended, out_weight) + out_bias
    mid = inputs_f + attn_scale * attn_branch
    normal_two, inv_two = norm_stats(mid)
    mlp_low = (normal_two * mlp_gain + mlp_shift).astype(BF16)
    up_pre = dot_nn(mlp_low, up_weight) + up_bias
    cdf = 0.5 * (1.0 + lax.erf(up_pre * 0.7071067811865476))
    slope = cdf + up_pre * (0.3989422804014327 * jnp.exp(-0.5 * up_pre * up_pre))
    activated = (up_pre * cdf).astype(BF16)
    mlp_branch = dot_nn(activated, down_weight) + down_bias
    output = (mid + mlp_scale * mlp_branch).astype(BF16)

    grad_output = cotangent.reshape(total_rows, width).astype(F32)
    grad_mlp = (mlp_scale * grad_output).astype(BF16)
    sum_mlp_scale = jnp.sum(grad_output * mlp_branch, axis=0)
    sum_down_bias = jnp.sum(grad_mlp.astype(F32), axis=0)
    down_blocks = dot_tn(grad_mlp, activated).astype(BF16)
    down_blocks = down_blocks.reshape(tok_size, width // tok_size, head_size, hidden // head_size)
    down_blocks = down_blocks.transpose(0, 2, 1, 3)
    grad_down = reduce_blocks(down_blocks, order_a, sizes).T

    grad_up = (slope * dot_nt(grad_mlp, down_weight)).astype(BF16)
    sum_up_bias = jnp.sum(grad_up.astype(F32), axis=0)
    up_blocks = dot_tn(mlp_low, grad_up).astype(BF16)
    up_blocks = up_blocks.reshape(head_size, width // head_size, tok_size, hidden // tok_size)
    up_blocks = up_blocks.transpose(2, 0, 1, 3)
    grad_up_weight = reduce_blocks(up_blocks, order_b, sizes)

    grad_normed_two = dot_nt(grad_up, up_weight)
    grad_norm_two, sum_mlp_gain, sum_mlp_shift = norm_backward(
        grad_normed_two, mlp_gain, normal_two, inv_two
    )
    grad_mid = grad_output + grad_norm_two
    sum_attn_scale = jnp.sum(grad_mid * attn_branch, axis=0)
    grad_attn = (attn_scale * grad_mid).astype(BF16)
    sum_out_bias = jnp.sum(grad_attn.astype(F32), axis=0)
    grad_attended = dot_nt(grad_attn, out_weight).astype(BF16)
    out_blocks = dot_tn(grad_attn, attended).astype(BF16)
    out_blocks = out_blocks.reshape(tok_size, width // tok_size, head_size, width // head_size)
    grad_out = reduce_blocks(out_blocks.transpose(0, 2, 1, 3), order_a, sizes).T

    early = jnp.concatenate(
        [
            sum_out_bias,
            sum_attn_scale,
            sum_mlp_gain,
            sum_mlp_shift,
            sum_up_bias,
            sum_down_bias,
            sum_mlp_scale,
        ]
    ).reshape(-1, LANES)
    early = reduce_small(early, order_a, sizes).reshape(-1)

    grad_parts = []
    for m in range(micro):
        own = qkv[m * rows : (m + 1) * rows]
        grad = grad_attended[m * rows : (m + 1) * rows]
        dq, dleft, dkv, dright = attention_backward(
            *bounds[m], halo_kv[0, m], own, halo_kv[1, m], grad
        )
        from_right = shift_left(dleft, head_size).astype(F32)
        from_left = shift_right(dright, head_size).astype(F32)
        dkv = (
            dkv
            + jnp.pad(from_left, ((0, rows - HALO), (0, 0)))
            + jnp.pad(from_right, ((rows - HALO, 0), (0, 0)))
        )
        grad_parts.append(jnp.concatenate([dq, dkv.astype(BF16)], axis=1))
    grad_projected = jnp.concatenate(grad_parts, axis=0)
    sum_qkv_bias = jnp.sum(grad_projected.astype(F32), axis=0)
    qkv_blocks = dot_tn(grad_projected, normed_low).astype(BF16)
    qkv_blocks = qkv_blocks.reshape(tok_size, 3 * width // tok_size, head_size, width // head_size)
    grad_qkv = reduce_blocks(qkv_blocks.transpose(0, 2, 1, 3), order_a, sizes).T
    grad_normed_one = dot_nt(grad_projected, qkv_weight)
    grad_norm_one, sum_attn_gain, sum_attn_shift = norm_backward(
        grad_normed_one, attn_gain, normal_one, inv_one
    )
    input_grad = grad_mid + grad_norm_one
    late = jnp.concatenate(
        [sum_attn_gain, sum_attn_shift, sum_qkv_bias[:width], sum_qkv_bias[2 * width :]]
    ).reshape(-1, LANES)
    late = reduce_small(late, order_a, sizes).reshape(-1)

    w = width
    return (
        output.reshape(micro, rows, width),
        input_grad.reshape(micro, rows, width),
        late[:w],
        late[w : 2 * w],
        grad_qkv,
        late[2 * w : 3 * w],
        late[3 * w :],
        grad_out,
        early[:w],
        early[w : 2 * w],
        early[2 * w : 3 * w],
        early[3 * w : 4 * w],
        grad_up_weight,
        early[4 * w : 4 * w + hidden],
        grad_down,
        early[4 * w + hidden : 5 * w + hidden],
        early[5 * w + hidden :],
    )


def solution(mesh):
    sizes = {"tok": mesh.shape["tok"], "head": mesh.shape["head"]}
    rows = P(None, ("tok", "head"), None)
    crops = P(None, "tok", None)
    whole = P()
    split = P("head", "tok")
    return jax.shard_map(
        partial(per_device, sizes),
        mesh=mesh,
        in_specs=(rows, crops, crops) + (whole,) * 15 + (rows,),
        out_specs=(
            rows,
            rows,
            whole,
            whole,
            split,
            whole,
            whole,
            split,
            whole,
            whole,
            whole,
            whole,
            split,
            whole,
            split,
            whole,
            whole,
        ),
        check_vma=False,
    )
```

```python
from functools import partial

import jax
import jax.numpy as jnp
from jax import lax
from jax.experimental import pallas as pl
from jax.experimental.pallas import tpu as pltpu
from jax.sharding import PartitionSpec as P

HEAD_DIM = 64
NORM_EPS = 1e-06
MASKED = -1e30
HALO = 272
QT = 128
LANES = 128
FF_BLOCK = 384
F32 = jnp.float32
BF16 = jnp.bfloat16


def norm_stats(values):
    center = jnp.mean(values, axis=-1, keepdims=True)
    centered = values - center
    variance = jnp.mean(centered * centered, axis=-1, keepdims=True)
    inv_std = lax.rsqrt(variance + NORM_EPS)
    return centered * inv_std, inv_std


def norm_backward(grad_out, gain, normal_rows, inv_std):
    scaled = grad_out * gain
    mean_one = jnp.mean(scaled, axis=-1, keepdims=True)
    mean_two = jnp.mean(scaled * normal_rows, axis=-1, keepdims=True)
    grad_in = inv_std * (scaled - mean_one - normal_rows * mean_two)
    return grad_in, jnp.sum(grad_out * normal_rows, axis=0), jnp.sum(grad_out, axis=0)


def dot_nn(a, b):
    return lax.dot_general(a, b, (((1,), (0,)), ((), ())), preferred_element_type=F32)


def dot_nt(a, b):
    return lax.dot_general(a, b, (((1,), (1,)), ((), ())), preferred_element_type=F32)


def dot_tn(a, b):
    return lax.dot_general(a, b, (((0,), (0,)), ((), ())), preferred_element_type=F32)


def crop_bounds(starts, lengths, first_row, rows, group_rows):
    row_ids = first_row + lax.iota(jnp.int32, rows)[:, None]
    ends = jnp.minimum(starts + lengths, group_rows)
    inside = (row_ids >= starts[None, :]) & (row_ids < ends[None, :])
    found = jnp.any(inside, axis=1)
    low = jnp.where(found, jnp.sum(jnp.where(inside, starts[None, :], 0), axis=1), row_ids[:, 0])
    high = jnp.where(found, jnp.sum(jnp.where(inside, ends[None, :], 0), axis=1), row_ids[:, 0] + 1)
    return low - first_row + HALO, high - first_row + HALO


def tile_ranges(low, high, window):
    tiles = low.shape[0] // QT
    first = (low.reshape(tiles, QT)[:, 0] // 16) * 16
    last = high.reshape(tiles, QT)[:, QT - 1]
    count = jnp.clip((last - first + LANES - 1) // LANES, 1, 6)
    first = jnp.clip(first, 0, window - count * LANES)
    return jnp.concatenate([first, count]).astype(jnp.int32)


def load_window(left, own, right, win, width):
    rows = own.shape[0]
    win[0:HALO, :] = left[...]
    win[HALO : HALO + rows, :] = own[:, width:]
    win[HALO + rows :, :] = right[...]


def pair_stack(values):
    lane = lax.broadcasted_iota(jnp.int32, values.shape, 1)
    zero = jnp.zeros_like(values)
    one = jnp.where(lane < HEAD_DIM, values, zero)
    two = jnp.where(lane < HEAD_DIM, zero, values)
    return jnp.concatenate([one, two], axis=0)


def pair_merge(values):
    half = values.shape[0] // 2
    lane = lax.broadcasted_iota(jnp.int32, (half, LANES), 1)
    return jnp.where(lane < HEAD_DIM, values[:half], values[half:])


def tile_bias(low_ref, high_ref, row0, first, span):
    cols = first + lax.broadcasted_iota(jnp.int32, (QT, span), 1)
    low = low_ref[pl.ds(row0, QT), :]
    high = high_ref[pl.ds(row0, QT), :]
    same = (cols >= low) & (cols < high)
    bias = jnp.where(same, 0.0, MASKED).astype(F32)
    return jnp.concatenate([bias, bias], axis=0)


def forward_kernel(ranges, low_ref, high_ref, left, own, right, out, win):
    width = out.shape[1]
    rows = own.shape[0]
    tiles = rows // QT
    load_window(left, own, right, win, width)

    def tile(i, carry):
        row0 = pl.multiple_of(i * QT, QT)
        first = pl.multiple_of(ranges[i], 16)
        count = ranges[tiles + i]
        for n in range(1, 7):

            @pl.when(count == n)
            def _():
                span = n * LANES
                bias = tile_bias(low_ref, high_ref, row0, first, span)

                def pair(p, inner):
                    col = pl.multiple_of(p * LANES, LANES)
                    vcol = pl.multiple_of(width + p * LANES, LANES)
                    query = own[pl.ds(row0, QT), pl.ds(col, LANES)]
                    stacked = pair_stack(query * jnp.asarray(0.125, BF16))
                    keys = win[pl.ds(first, span), pl.ds(col, LANES)]
                    scores = dot_nt(stacked, keys) + bias
                    peak = jnp.max(scores, axis=1, keepdims=True)
                    expo = jnp.exp(scores - peak)
                    total = jnp.sum(expo, axis=1, keepdims=True)
                    vals = win[pl.ds(first, span), pl.ds(vcol, LANES)]
                    res = dot_nn(expo.astype(BF16), vals) / total
                    out[pl.ds(row0, QT), pl.ds(col, LANES)] = pair_merge(res).astype(BF16)
                    return inner

                lax.fori_loop(0, width // LANES, pair, 0)

        return carry

    lax.fori_loop(0, tiles, tile, 0)


def backward_kernel(
    ranges, low_ref, high_ref, left, own, right, grad, dq, dleft, down, dright, win, acc
):
    width = grad.shape[1]
    rows = own.shape[0]
    tiles = rows // QT
    load_window(left, own, right, win, width)
    acc[...] = jnp.zeros_like(acc)

    def tile(i, carry):
        row0 = pl.multiple_of(i * QT, QT)
        first = pl.multiple_of(ranges[i], 16)
        count = ranges[tiles + i]
        for n in range(1, 7):

            @pl.when(count == n)
            def _():
                span = n * LANES
                bias = tile_bias(low_ref, high_ref, row0, first, span)

                def pair(p, inner):
                    col = pl.multiple_of(p * LANES, LANES)
                    vcol = pl.multiple_of(width + p * LANES, LANES)
                    query = own[pl.ds(row0, QT), pl.ds(col, LANES)]
                    stacked = pair_stack(query * jnp.asarray(0.125, BF16))
                    gstack = pair_stack(grad[pl.ds(row0, QT), pl.ds(col, LANES)])
                    keys = win[pl.ds(first, span), pl.ds(col, LANES)]
                    vals = win[pl.ds(first, span), pl.ds(vcol, LANES)]
                    scores = dot_nt(stacked, keys) + bias
                    peak = jnp.max(scores, axis=1, keepdims=True)
                    expo = jnp.exp(scores - peak)
                    total = jnp.sum(expo, axis=1, keepdims=True)
                    probs = expo * (1.0 / total)
                    dprobs = dot_nt(gstack, vals)
                    row_dot = jnp.sum(probs * dprobs, axis=1, keepdims=True)
                    dscores = (probs * (dprobs - row_dot)).astype(BF16)
                    res = dot_nn(dscores, keys) * 0.125
                    dq[pl.ds(row0, QT), pl.ds(col, LANES)] = pair_merge(res).astype(BF16)
                    acc[pl.ds(first, span), pl.ds(col, LANES)] += dot_tn(dscores, stacked)
                    acc[pl.ds(first, span), pl.ds(vcol, LANES)] += dot_tn(
                        probs.astype(BF16), gstack
                    )
                    return inner

                lax.fori_loop(0, width // LANES, pair, 0)

        return carry

    lax.fori_loop(0, tiles, tile, 0)
    dleft[...] = acc[0:HALO, :].astype(BF16)
    down[...] = acc[HALO : HALO + rows, :]
    dright[...] = acc[HALO + rows :, :].astype(BF16)


def smem():
    return pl.BlockSpec(memory_space=pltpu.SMEM)


def vmem():
    return pl.BlockSpec(memory_space=pltpu.VMEM)


def attention_forward(ranges, low, high, left, own, right):
    rows, width = own.shape[0], own.shape[1] // 3
    window = rows + 2 * HALO
    return pl.pallas_call(
        forward_kernel,
        out_shape=jax.ShapeDtypeStruct((rows, width), BF16),
        in_specs=[smem()] + [vmem()] * 5,
        out_specs=vmem(),
        scratch_shapes=[pltpu.VMEM((window, 2 * width), BF16)],
        cost_estimate=pl.CostEstimate(
            flops=4 * rows * 640 * width * 4, bytes_accessed=8 * 1024 * 1024, transcendentals=0
        ),
        name="attn_fwd",
    )(ranges, low, high, left, own, right)


def attention_backward(ranges, low, high, left, own, right, grad):
    rows, width = grad.shape
    window = rows + 2 * HALO
    return pl.pallas_call(
        backward_kernel,
        out_shape=(
            jax.ShapeDtypeStruct((rows, width), BF16),
            jax.ShapeDtypeStruct((HALO, 2 * width), BF16),
            jax.ShapeDtypeStruct((rows, 2 * width), F32),
            jax.ShapeDtypeStruct((HALO, 2 * width), BF16),
        ),
        in_specs=[smem()] + [vmem()] * 6,
        out_specs=(vmem(),) * 4,
        scratch_shapes=[
            pltpu.VMEM((window, 2 * width), BF16),
            pltpu.VMEM((window, 2 * width), F32),
        ],
        cost_estimate=pl.CostEstimate(
            flops=10 * rows * 640 * width * 4, bytes_accessed=16 * 1024 * 1024, transcendentals=0
        ),
        name="attn_bwd",
    )(ranges, low, high, left, own, right, grad)


def column_sum(values):
    return jnp.sum(values, axis=0, keepdims=True)


def mlp_kernel(
    attended,
    tokens,
    cotangent,
    out_weight,
    vectors,
    up_weight,
    up_bias,
    down_weight,
    output,
    grad_mid,
    grad_attn,
    grad_attended,
    small,
    up_grad,
    down_grad,
    up_bias_grad,
    mid,
    normal,
    inv_std,
    branch,
    low,
    grad_mlp,
    acc,
    err,
):
    step = pl.program_id(0)
    out_bias, attn_scale = vectors[0:1, :], vectors[1:2, :]
    gain, shift = vectors[2:3, :], vectors[3:4, :]
    mlp_scale, down_bias = vectors[4:5, :], vectors[5:6, :]

    @pl.when(step == 0)
    def _():
        first = dot_nn(attended[...], out_weight[...]) + out_bias
        branch[...] = first
        total = tokens[...].astype(F32) + attn_scale * first
        mid[...] = total
        rows_n, inv = norm_stats(total)
        normal[...] = rows_n
        inv_std[...] = inv
        low[...] = (rows_n * gain + shift).astype(BF16)
        grad_mlp[...] = (mlp_scale * cotangent[...].astype(F32)).astype(BF16)
        acc[...] = jnp.zeros_like(acc)
        err[...] = jnp.zeros_like(err)

    up_pre = dot_nn(low[...], up_weight[...]) + up_bias[...]
    cdf = 0.5 * (1.0 + lax.erf(up_pre * 0.7071067811865476))
    slope = cdf + up_pre * (0.3989422804014327 * jnp.exp(-0.5 * up_pre * up_pre))
    active = (up_pre * cdf).astype(BF16)
    grad_up = (slope * dot_nt(grad_mlp[...], down_weight[...])).astype(BF16)
    acc[...] += dot_nn(active, down_weight[...])
    err[...] += dot_nt(grad_up, up_weight[...])
    up_bias_grad[...] = column_sum(grad_up.astype(F32))
    up_grad[...] = dot_tn(low[...], grad_up).astype(BF16).reshape(up_grad.shape)
    down_grad[...] = dot_tn(grad_mlp[...], active).astype(BF16).reshape(down_grad.shape)

    @pl.when(step == pl.num_programs(0) - 1)
    def _():
        grad_out = cotangent[...].astype(F32)
        mlp_branch = acc[...] + down_bias
        output[...] = (mid[...] + mlp_scale * mlp_branch).astype(BF16)
        e = err[...]
        rows_n = normal[...]
        scaled = e * gain
        mean_one = jnp.mean(scaled, axis=-1, keepdims=True)
        mean_two = jnp.mean(scaled * rows_n, axis=-1, keepdims=True)
        total = grad_out + inv_std[...] * (scaled - mean_one - rows_n * mean_two)
        grad_mid[...] = total
        low_grad = (attn_scale * total).astype(BF16)
        grad_attn[...] = low_grad
        grad_attended[...] = dot_nt(low_grad, out_weight[...]).astype(BF16)
        small[0:1, :] = column_sum(low_grad.astype(F32))
        small[1:2, :] = column_sum(total * branch[...])
        small[2:3, :] = column_sum(e * rows_n)
        small[3:4, :] = column_sum(e)
        small[4:5, :] = column_sum(grad_mlp[...].astype(F32))
        small[5:6, :] = column_sum(grad_out * mlp_branch)
        small[6:8, :] = jnp.zeros((2, small.shape[1]), F32)


def mlp_call(attended, tokens, cotangent, out_weight, vectors, up_weight, up_bias, down_weight):
    rows, width = tokens.shape
    hidden = up_weight.shape[1]
    steps = hidden // FF_BLOCK
    cut = width // 8
    fixed = lambda shape: pl.BlockSpec(shape, lambda j: (0,) * len(shape))
    return pl.pallas_call(
        mlp_kernel,
        grid=(steps,),
        in_specs=[
            fixed((rows, width)),
            fixed((rows, width)),
            fixed((rows, width)),
            fixed((width, width)),
            fixed((8, width)),
            pl.BlockSpec((width, FF_BLOCK), lambda j: (0, j)),
            pl.BlockSpec((1, FF_BLOCK), lambda j: (0, j)),
            pl.BlockSpec((FF_BLOCK, width), lambda j: (j, 0)),
        ],
        out_specs=(
            fixed((rows, width)),
            fixed((rows, width)),
            fixed((rows, width)),
            fixed((rows, width)),
            fixed((8, width)),
            pl.BlockSpec((1, 4, width // 4, FF_BLOCK), lambda j: (j, 0, 0, 0)),
            pl.BlockSpec((8, 1, 1, cut, FF_BLOCK), lambda j: (0, j // 2, j % 2, 0, 0)),
            pl.BlockSpec((1, FF_BLOCK), lambda j: (0, j)),
        ),
        out_shape=(
            jax.ShapeDtypeStruct((rows, width), BF16),
            jax.ShapeDtypeStruct((rows, width), F32),
            jax.ShapeDtypeStruct((rows, width), BF16),
            jax.ShapeDtypeStruct((rows, width), BF16),
            jax.ShapeDtypeStruct((8, width), F32),
            jax.ShapeDtypeStruct((8, 4, width // 4, FF_BLOCK), BF16),
            jax.ShapeDtypeStruct((8, 4, 2, cut, FF_BLOCK), BF16),
            jax.ShapeDtypeStruct((1, hidden), F32),
        ),
        scratch_shapes=[
            pltpu.VMEM((rows, width), F32),
            pltpu.VMEM((rows, width), F32),
            pltpu.VMEM((rows, 1), F32),
            pltpu.VMEM((rows, width), F32),
            pltpu.VMEM((rows, width), BF16),
            pltpu.VMEM((rows, width), BF16),
            pltpu.VMEM((rows, width), F32),
            pltpu.VMEM((rows, width), F32),
        ],
        cost_estimate=pl.CostEstimate(
            flops=12 * rows * width * hidden, bytes_accessed=32 * 1024 * 1024, transcendentals=0
        ),
        name="mlp_both",
    )(attended, tokens, cotangent, out_weight, vectors, up_weight, up_bias, down_weight)


def grads_kernel(
    dq0, dq1, own0, own1, fl0, fl1, fr0, fr1, normed, gattn, attended,
    gproj, one, two, sums, acc, wt, og,
):
    rows, width = dq0.shape
    for m, (dq, own, left, right) in enumerate(
        ((dq0, own0, fl0, fr0), (dq1, own1, fl1, fr1))
    ):
        acc[...] = own[...]
        acc[0:HALO, :] += left[...].astype(F32)
        acc[rows - HALO :, :] += right[...].astype(F32)
        gproj[m * rows : (m + 1) * rows, 0:width] = dq[...]
        gproj[m * rows : (m + 1) * rows, width:] = acc[...].astype(BF16)
    og[...] = dot_tn(gattn[...], attended[...])
    cols = 3 * width // 8
    cut = width // 8
    half = (cols + cut) // 2
    lane = lax.broadcasted_iota(jnp.int32, (half, 2 * (width // 4)), 1)
    first = lane < width // 4
    for k in range(2):
        part = gproj[:, 4 * cols * k : 4 * cols * (k + 1)]
        sums[:, 4 * cols * k : 4 * cols * (k + 1)] = column_sum(part.astype(F32))
        wt[...] = dot_tn(part, normed[...])
        for tt in range(4):
            t = 4 * k + tt
            for x in range(2):
                span = slice(2 * (width // 4) * x, 2 * (width // 4) * (x + 1))
                top = wt[cols * tt : cols * tt + half, span]
                bottom = jnp.concatenate(
                    [wt[cols * tt + half : cols * (tt + 1), span], og[cut * t : cut * (t + 1), span]],
                    axis=0,
                )
                even = jnp.where(first, top, pltpu.roll(bottom, width // 4, 1)).astype(BF16)
                odd = jnp.where(first, pltpu.roll(top, width // 4, 1), bottom).astype(BF16)
                one[t, 2 * x] = even[: half // 2]
                two[t, 2 * x] = even[half // 2 :]
                one[t, 2 * x + 1] = odd[: half // 2]
                two[t, 2 * x + 1] = odd[half // 2 :]


def grads_call(*operands):
    rows, width = operands[0].shape
    total = operands[8].shape[0]
    shape = (8, 4, width // 8, width // 2)
    return pl.pallas_call(
        grads_kernel,
        in_specs=[vmem()] * 11,
        out_specs=(vmem(),) * 4,
        out_shape=(
            jax.ShapeDtypeStruct((total, 3 * width), BF16),
            jax.ShapeDtypeStruct(shape, BF16),
            jax.ShapeDtypeStruct(shape, BF16),
            jax.ShapeDtypeStruct((1, 3 * width), F32),
        ),
        scratch_shapes=[
            pltpu.VMEM((rows, 2 * width), F32),
            pltpu.VMEM((3 * width // 2, width), F32),
            pltpu.VMEM((width, width), F32),
        ],
        cost_estimate=pl.CostEstimate(
            flops=8 * total * width * width, bytes_accessed=24 * 1024 * 1024, transcendentals=0
        ),
        name="qkv_grads",
    )(*operands)


def shift_right(values, size):
    return lax.ppermute(values, "head", [(i, i + 1) for i in range(size - 1)])


def shift_left(values, size):
    return lax.ppermute(values, "head", [(i + 1, i) for i in range(size - 1)])


def axis_bits(size):
    return size.bit_length() - 1


def bit_orders(tok_size, head_size):
    tok = [("tok", b) for b in range(axis_bits(tok_size))]
    head = [("head", b) for b in range(axis_bits(head_size))]
    return head + tok, head[:1] + tok + head[1:]


def swap_pairs(size, bit):
    return [(i, i ^ (1 << bit)) for i in range(size)]


class BlockSum:
    def __init__(self, blocks, order, sizes):
        self.dims = [("tok", b) for b in reversed(range(axis_bits(sizes["tok"])))]
        self.dims += [("head", b) for b in reversed(range(axis_bits(sizes["head"])))]
        self.part = blocks.reshape((2,) * len(self.dims) + blocks.shape[2:])
        self.order = list(order)
        self.sizes = sizes
        self.flight = None

    def start(self):
        axis, bit = self.order.pop(0)
        where = self.dims.index((axis, bit))
        mine = (lax.axis_index(axis) >> bit) & 1
        send = lax.dynamic_index_in_dim(self.part, 1 - mine, where, keepdims=False)
        keep = lax.dynamic_index_in_dim(self.part, mine, where, keepdims=False)
        got = lax.ppermute(send, axis, swap_pairs(self.sizes[axis], bit))
        self.flight = (keep, got)
        self.dims.pop(where)

    def finish(self):
        keep, got = self.flight
        part = keep.astype(F32) + got.astype(F32)
        self.part = part.astype(BF16) if self.order else part
        return self.part

    def run(self):
        while self.order:
            self.start()
            self.finish()
        return self.part


def reduce_small(values, order, sizes):
    for axis, bit in order:
        values = values + lax.ppermute(values, axis, swap_pairs(sizes[axis], bit))
    return values


def per_device(
    sizes,
    tokens,
    crop_start,
    crop_len,
    attn_gain,
    attn_shift,
    qkv_weight,
    query_bias,
    value_bias,
    out_weight,
    out_bias,
    attn_scale,
    mlp_gain,
    mlp_shift,
    up_weight,
    up_bias,
    down_weight,
    down_bias,
    mlp_scale,
    cotangent,
):
    micro, rows, width = tokens.shape
    hidden = up_weight.shape[1]
    tok_size, head_size = sizes["tok"], sizes["head"]
    window = rows + 2 * HALO
    head_at = lax.axis_index("head")
    order_a, order_b = bit_orders(tok_size, head_size)
    kv_bias = jnp.concatenate([jnp.zeros_like(value_bias), value_bias])
    qkv_bias = jnp.concatenate([query_bias, kv_bias])

    halo_left = shift_right(tokens[:, rows - HALO :, :], head_size)
    halo_right = shift_left(tokens[:, :HALO, :], head_size)

    total_rows = micro * rows
    inputs_f = tokens.reshape(total_rows, width).astype(F32)
    normal_one, inv_one = norm_stats(inputs_f)
    normed_low = (normal_one * attn_gain + attn_shift).astype(BF16)
    qkv = (dot_nn(normed_low, qkv_weight) + qkv_bias).astype(BF16)

    halo = jnp.stack([halo_left, halo_right]).reshape(2 * micro * HALO, width)
    halo_normal, _ = norm_stats(halo.astype(F32))
    halo_low = (halo_normal * attn_gain + attn_shift).astype(BF16)
    halo_kv = (dot_nn(halo_low, qkv_weight[:, width:]) + kv_bias).astype(BF16)
    halo_kv = halo_kv.reshape(2, micro, HALO, 2 * width)

    bounds = []
    attended_parts = []
    for m in range(micro):
        low, high = crop_bounds(
            crop_start[m, 0], crop_len[m, 0], head_at * rows, rows, head_size * rows
        )
        ranges = tile_ranges(low, high, window)
        bounds.append((ranges, low[:, None], high[:, None]))
        own = qkv[m * rows : (m + 1) * rows]
        attended_parts.append(attention_forward(*bounds[m], halo_kv[0, m], own, halo_kv[1, m]))
    attended = jnp.concatenate(attended_parts, axis=0)

    vectors = jnp.stack(
        [
            out_bias,
            attn_scale,
            mlp_gain,
            mlp_shift,
            mlp_scale,
            down_bias,
            jnp.zeros_like(out_bias),
            jnp.zeros_like(out_bias),
        ]
    )
    output, grad_mid, grad_attn, grad_attended, small, up_blocks, down_blocks, sum_up_bias = mlp_call(
        attended,
        tokens.reshape(total_rows, width),
        cotangent.reshape(total_rows, width),
        out_weight,
        vectors,
        up_weight,
        up_bias[None, :],
        down_weight,
    )
    more = tok_size // 8
    if more > 1:
        up_blocks = up_blocks.reshape(8, 4, width // 4, more, -1).transpose(0, 3, 1, 2, 4)
        up_blocks = up_blocks.reshape((tok_size,) + up_blocks.shape[2:])
        down_blocks = down_blocks.reshape(8, 4, 2, more, -1, FF_BLOCK).transpose(0, 3, 1, 2, 4, 5)
        down_blocks = down_blocks.reshape((tok_size,) + down_blocks.shape[2:])
    up_sum = BlockSum(up_blocks, order_b, sizes)
    down_sum = BlockSum(down_blocks, order_a, sizes)

    grads = []
    for m in range(micro):
        up_sum.start()
        down_sum.start()
        own = qkv[m * rows : (m + 1) * rows]
        grad = grad_attended[m * rows : (m + 1) * rows]
        dq, dleft, dkv, dright = attention_backward(
            *bounds[m], halo_kv[0, m], own, halo_kv[1, m], grad
        )
        up_sum.finish()
        down_sum.finish()
        grads.append((dq, dkv, shift_right(dright, head_size), shift_left(dleft, head_size)))
    (dq0, own0, fl0, fr0), (dq1, own1, fl1, fr1) = grads
    grad_projected, one, two, sum_qkv_bias = grads_call(
        dq0, dq1, own0, own1, fl0, fl1, fr0, fr1, normed_low, grad_attn, attended
    )
    if more > 1:
        whole = jnp.concatenate([one, two], axis=2)
        tall = jnp.concatenate(jnp.split(whole, 2, axis=3), axis=2)
        cols = 3 * width // 8
        pieces = [tall[:, :, :cols], tall[:, :, cols:]]
        pieces = [p.reshape(8, 4, more, -1, width // 4).transpose(0, 2, 1, 3, 4) for p in pieces]
        tall = jnp.concatenate(pieces, axis=3)
        tall = tall.reshape((tok_size,) + tall.shape[2:])
        half = tall.shape[2] // 2
        one, two = tall[:, :, :half], tall[:, :, half:]
    one = BlockSum(one, order_a, sizes).run()
    two = BlockSum(two, order_b, sizes).run()
    tall = jnp.concatenate([one, two], axis=0)
    if more == 1:
        tall = jnp.concatenate(jnp.split(tall, 2, axis=1), axis=0)
    grad_qkv = tall[: 3 * width // tok_size].T
    grad_out = tall[3 * width // tok_size :].T
    grad_up_weight = up_sum.run()
    grad_down = down_sum.run()
    grad_down = grad_down.transpose(0, 2, 1).reshape(hidden // head_size, width // tok_size)

    grad_normed_one = dot_nt(grad_projected, qkv_weight)
    grad_norm_one, sum_attn_gain, sum_attn_shift = norm_backward(
        grad_normed_one, attn_gain, normal_one, inv_one
    )
    input_grad = grad_mid + grad_norm_one
    w = width
    sum_qkv_bias = sum_qkv_bias.reshape(-1)
    vecs = jnp.concatenate(
        [
            small[:6].reshape(-1),
            sum_up_bias.reshape(-1),
            sum_attn_gain,
            sum_attn_shift,
            sum_qkv_bias[:w],
            sum_qkv_bias[2 * w :],
        ]
    ).reshape(-1, LANES)
    vecs = reduce_small(vecs, order_a, sizes).reshape(-1)
    early = vecs[: 6 * w].reshape(6, w)
    late = vecs[6 * w + hidden :].reshape(4, w)
    return (
        output.reshape(micro, rows, width),
        input_grad.reshape(micro, rows, width),
        late[0],
        late[1],
        grad_qkv,
        late[2],
        late[3],
        grad_out,
        early[0],
        early[1],
        early[2],
        early[3],
        grad_up_weight,
        vecs[6 * w : 6 * w + hidden],
        grad_down,
        early[4],
        early[5],
    )


def solution(mesh):
    sizes = {"tok": mesh.shape["tok"], "head": mesh.shape["head"]}
    rows = P(None, ("tok", "head"), None)
    crops = P(None, "tok", None)
    whole = P()
    split = P("head", "tok")
    return jax.shard_map(
        partial(per_device, sizes),
        mesh=mesh,
        in_specs=(rows, crops, crops) + (whole,) * 15 + (rows,),
        out_specs=(
            rows,
            rows,
            whole,
            whole,
            split,
            whole,
            whole,
            split,
            whole,
            whole,
            whole,
            whole,
            split,
            whole,
            split,
            whole,
            whole,
        ),
        check_vma=False,
    )
```

```python
from functools import partial

import jax
import jax.numpy as jnp
from jax import lax
from jax.experimental import pallas as pl
from jax.experimental.pallas import tpu as pltpu
from jax.sharding import PartitionSpec as P

HEAD_DIM = 64
NORM_EPS = 1e-06
MASKED = -1e30
HALO = 272
QT = 128
LANES = 128
FF_BLOCK = 384
F32 = jnp.float32
BF16 = jnp.bfloat16


def norm_stats(values):
    center = jnp.mean(values, axis=-1, keepdims=True)
    centered = values - center
    variance = jnp.mean(centered * centered, axis=-1, keepdims=True)
    inv_std = lax.rsqrt(variance + NORM_EPS)
    return centered * inv_std, inv_std


def norm_backward(grad_out, gain, normal_rows, inv_std):
    scaled = grad_out * gain
    mean_one = jnp.mean(scaled, axis=-1, keepdims=True)
    mean_two = jnp.mean(scaled * normal_rows, axis=-1, keepdims=True)
    grad_in = inv_std * (scaled - mean_one - normal_rows * mean_two)
    return grad_in, jnp.sum(grad_out * normal_rows, axis=0), jnp.sum(grad_out, axis=0)


def dot_nn(a, b):
    return lax.dot_general(a, b, (((1,), (0,)), ((), ())), preferred_element_type=F32)


def dot_nt(a, b):
    return lax.dot_general(a, b, (((1,), (1,)), ((), ())), preferred_element_type=F32)


def dot_tn(a, b):
    return lax.dot_general(a, b, (((0,), (0,)), ((), ())), preferred_element_type=F32)


def crop_bounds(starts, lengths, first_row, rows, group_rows):
    row_ids = first_row + lax.iota(jnp.int32, rows)[:, None]
    ends = jnp.minimum(starts + lengths, group_rows)
    inside = (row_ids >= starts[None, :]) & (row_ids < ends[None, :])
    found = jnp.any(inside, axis=1)
    low = jnp.where(found, jnp.sum(jnp.where(inside, starts[None, :], 0), axis=1), row_ids[:, 0])
    high = jnp.where(found, jnp.sum(jnp.where(inside, ends[None, :], 0), axis=1), row_ids[:, 0] + 1)
    return low - first_row + HALO, high - first_row + HALO


def tile_ranges(low, high, window):
    tiles = low.shape[0] // QT
    first = (low.reshape(tiles, QT)[:, 0] // 16) * 16
    last = high.reshape(tiles, QT)[:, QT - 1]
    count = jnp.clip((last - first + LANES - 1) // LANES, 1, 6)
    first = jnp.clip(first, 0, window - count * LANES)
    return jnp.concatenate([first, count]).astype(jnp.int32)


def load_window(left, own, right, win, width):
    rows = own.shape[0]
    win[0:HALO, :] = left[...]
    win[HALO : HALO + rows, :] = own[:, width:]
    win[HALO + rows :, :] = right[...]


def pair_stack(values):
    lane = lax.broadcasted_iota(jnp.int32, values.shape, 1)
    zero = jnp.zeros_like(values)
    one = jnp.where(lane < HEAD_DIM, values, zero)
    two = jnp.where(lane < HEAD_DIM, zero, values)
    return jnp.concatenate([one, two], axis=0)


def pair_merge(values):
    half = values.shape[0] // 2
    lane = lax.broadcasted_iota(jnp.int32, (half, LANES), 1)
    return jnp.where(lane < HEAD_DIM, values[:half], values[half:])


def tile_bias(low_ref, high_ref, row0, first, span):
    cols = first + lax.broadcasted_iota(jnp.int32, (QT, span), 1)
    low = low_ref[pl.ds(row0, QT), :]
    high = high_ref[pl.ds(row0, QT), :]
    same = (cols >= low) & (cols < high)
    bias = jnp.where(same, 0.0, MASKED).astype(F32)
    return jnp.concatenate([bias, bias], axis=0)


def forward_kernel(ranges, low_ref, high_ref, left, own, right, out, win):
    width = out.shape[1]
    rows = own.shape[0]
    tiles = rows // QT
    load_window(left, own, right, win, width)

    def tile(i, carry):
        row0 = pl.multiple_of(i * QT, QT)
        first = pl.multiple_of(ranges[i], 16)
        count = ranges[tiles + i]
        for n in range(1, 7):

            @pl.when(count == n)
            def _():
                span = n * LANES
                bias = tile_bias(low_ref, high_ref, row0, first, span)

                def pair(p, inner):
                    col = pl.multiple_of(p * LANES, LANES)
                    vcol = pl.multiple_of(width + p * LANES, LANES)
                    query = own[pl.ds(row0, QT), pl.ds(col, LANES)]
                    stacked = pair_stack(query * jnp.asarray(0.125, BF16))
                    keys = win[pl.ds(first, span), pl.ds(col, LANES)]
                    scores = dot_nt(stacked, keys) + bias
                    peak = jnp.max(scores, axis=1, keepdims=True)
                    expo = jnp.exp(scores - peak)
                    total = jnp.sum(expo, axis=1, keepdims=True)
                    vals = win[pl.ds(first, span), pl.ds(vcol, LANES)]
                    res = dot_nn(expo.astype(BF16), vals) / total
                    out[pl.ds(row0, QT), pl.ds(col, LANES)] = pair_merge(res).astype(BF16)
                    return inner

                lax.fori_loop(0, width // LANES, pair, 0)

        return carry

    lax.fori_loop(0, tiles, tile, 0)


def backward_kernel(
    ranges, low_ref, high_ref, left, own, right, grad, dq, dleft, down, dright, win, acc
):
    width = grad.shape[1]
    rows = own.shape[0]
    tiles = rows // QT
    load_window(left, own, right, win, width)
    acc[...] = jnp.zeros_like(acc)

    def tile(i, carry):
        row0 = pl.multiple_of(i * QT, QT)
        first = pl.multiple_of(ranges[i], 16)
        count = ranges[tiles + i]
        for n in range(1, 7):

            @pl.when(count == n)
            def _():
                span = n * LANES
                bias = tile_bias(low_ref, high_ref, row0, first, span)

                def pair(p, inner):
                    col = pl.multiple_of(p * LANES, LANES)
                    vcol = pl.multiple_of(width + p * LANES, LANES)
                    query = own[pl.ds(row0, QT), pl.ds(col, LANES)]
                    stacked = pair_stack(query * jnp.asarray(0.125, BF16))
                    gstack = pair_stack(grad[pl.ds(row0, QT), pl.ds(col, LANES)])
                    keys = win[pl.ds(first, span), pl.ds(col, LANES)]
                    vals = win[pl.ds(first, span), pl.ds(vcol, LANES)]
                    scores = dot_nt(stacked, keys) + bias
                    peak = jnp.max(scores, axis=1, keepdims=True)
                    expo = jnp.exp(scores - peak)
                    total = jnp.sum(expo, axis=1, keepdims=True)
                    probs = expo * (1.0 / total)
                    dprobs = dot_nt(gstack, vals)
                    row_dot = jnp.sum(probs * dprobs, axis=1, keepdims=True)
                    dscores = (probs * (dprobs - row_dot)).astype(BF16)
                    res = dot_nn(dscores, keys) * 0.125
                    dq[pl.ds(row0, QT), pl.ds(col, LANES)] = pair_merge(res).astype(BF16)
                    acc[pl.ds(first, span), pl.ds(col, LANES)] += dot_tn(dscores, stacked)
                    acc[pl.ds(first, span), pl.ds(vcol, LANES)] += dot_tn(
                        probs.astype(BF16), gstack
                    )
                    return inner

                lax.fori_loop(0, width // LANES, pair, 0)

        return carry

    lax.fori_loop(0, tiles, tile, 0)
    dleft[...] = acc[0:HALO, :].astype(BF16)
    down[...] = acc[HALO : HALO + rows, :]
    dright[...] = acc[HALO + rows :, :].astype(BF16)


def smem():
    return pl.BlockSpec(memory_space=pltpu.SMEM)


def vmem():
    return pl.BlockSpec(memory_space=pltpu.VMEM)


def attention_forward(ranges, low, high, left, own, right):
    rows, width = own.shape[0], own.shape[1] // 3
    window = rows + 2 * HALO
    return pl.pallas_call(
        forward_kernel,
        out_shape=jax.ShapeDtypeStruct((rows, width), BF16),
        in_specs=[smem()] + [vmem()] * 5,
        out_specs=vmem(),
        scratch_shapes=[pltpu.VMEM((window, 2 * width), BF16)],
        cost_estimate=pl.CostEstimate(
            flops=4 * rows * 640 * width * 4, bytes_accessed=8 * 1024 * 1024, transcendentals=0
        ),
        name="attn_fwd",
    )(ranges, low, high, left, own, right)


def attention_backward(ranges, low, high, left, own, right, grad):
    rows, width = grad.shape
    window = rows + 2 * HALO
    return pl.pallas_call(
        backward_kernel,
        out_shape=(
            jax.ShapeDtypeStruct((rows, width), BF16),
            jax.ShapeDtypeStruct((HALO, 2 * width), BF16),
            jax.ShapeDtypeStruct((rows, 2 * width), F32),
            jax.ShapeDtypeStruct((HALO, 2 * width), BF16),
        ),
        in_specs=[smem()] + [vmem()] * 6,
        out_specs=(vmem(),) * 4,
        scratch_shapes=[
            pltpu.VMEM((window, 2 * width), BF16),
            pltpu.VMEM((window, 2 * width), F32),
        ],
        cost_estimate=pl.CostEstimate(
            flops=10 * rows * 640 * width * 4, bytes_accessed=16 * 1024 * 1024, transcendentals=0
        ),
        name="attn_bwd",
    )(ranges, low, high, left, own, right, grad)


def column_sum(values):
    return jnp.sum(values, axis=0, keepdims=True)


def mlp_kernel(
    attended,
    tokens,
    cotangent,
    out_weight,
    vectors,
    up_weight,
    up_bias,
    down_weight,
    output,
    grad_mid,
    grad_attn,
    grad_attended,
    small,
    up_grad,
    down_grad,
    up_bias_grad,
    mid,
    normal,
    inv_std,
    branch,
    low,
    grad_mlp,
    acc,
    err,
):
    step = pl.program_id(0)
    out_bias, attn_scale = vectors[0:1, :], vectors[1:2, :]
    gain, shift = vectors[2:3, :], vectors[3:4, :]
    mlp_scale, down_bias = vectors[4:5, :], vectors[5:6, :]

    @pl.when(step == 0)
    def _():
        first = dot_nn(attended[...], out_weight[...]) + out_bias
        branch[...] = first
        total = tokens[...].astype(F32) + attn_scale * first
        mid[...] = total
        rows_n, inv = norm_stats(total)
        normal[...] = rows_n
        inv_std[...] = inv
        low[...] = (rows_n * gain + shift).astype(BF16)
        grad_mlp[...] = (mlp_scale * cotangent[...].astype(F32)).astype(BF16)
        acc[...] = jnp.zeros_like(acc)
        err[...] = jnp.zeros_like(err)

    up_pre = dot_nn(low[...], up_weight[...]) + up_bias[...]
    cdf = 0.5 * (1.0 + lax.erf(up_pre * 0.7071067811865476))
    slope = cdf + up_pre * (0.3989422804014327 * jnp.exp(-0.5 * up_pre * up_pre))
    active = (up_pre * cdf).astype(BF16)
    grad_up = (slope * dot_nt(grad_mlp[...], down_weight[...])).astype(BF16)
    acc[...] += dot_nn(active, down_weight[...])
    err[...] += dot_nt(grad_up, up_weight[...])
    up_bias_grad[...] = column_sum(grad_up.astype(F32))
    up_grad[...] = dot_tn(low[...], grad_up).astype(BF16).reshape(up_grad.shape)
    down_grad[...] = dot_tn(grad_mlp[...], active).astype(BF16).reshape(down_grad.shape)

    @pl.when(step == pl.num_programs(0) - 1)
    def _():
        grad_out = cotangent[...].astype(F32)
        mlp_branch = acc[...] + down_bias
        output[...] = (mid[...] + mlp_scale * mlp_branch).astype(BF16)
        e = err[...]
        rows_n = normal[...]
        scaled = e * gain
        mean_one = jnp.mean(scaled, axis=-1, keepdims=True)
        mean_two = jnp.mean(scaled * rows_n, axis=-1, keepdims=True)
        total = grad_out + inv_std[...] * (scaled - mean_one - rows_n * mean_two)
        grad_mid[...] = total
        low_grad = (attn_scale * total).astype(BF16)
        grad_attn[...] = low_grad
        grad_attended[...] = dot_nt(low_grad, out_weight[...]).astype(BF16)
        small[0:1, :] = column_sum(low_grad.astype(F32))
        small[1:2, :] = column_sum(total * branch[...])
        small[2:3, :] = column_sum(e * rows_n)
        small[3:4, :] = column_sum(e)
        small[4:5, :] = column_sum(grad_mlp[...].astype(F32))
        small[5:6, :] = column_sum(grad_out * mlp_branch)
        small[6:8, :] = jnp.zeros((2, small.shape[1]), F32)


def mlp_call(attended, tokens, cotangent, out_weight, vectors, up_weight, up_bias, down_weight):
    rows, width = tokens.shape
    hidden = up_weight.shape[1]
    steps = hidden // FF_BLOCK
    cut = width // 8
    fixed = lambda shape: pl.BlockSpec(shape, lambda j: (0,) * len(shape))
    return pl.pallas_call(
        mlp_kernel,
        grid=(steps,),
        in_specs=[
            fixed((rows, width)),
            fixed((rows, width)),
            fixed((rows, width)),
            fixed((width, width)),
            fixed((8, width)),
            pl.BlockSpec((width, FF_BLOCK), lambda j: (0, j)),
            pl.BlockSpec((1, FF_BLOCK), lambda j: (0, j)),
            pl.BlockSpec((FF_BLOCK, width), lambda j: (j, 0)),
        ],
        out_specs=(
            fixed((rows, width)),
            fixed((rows, width)),
            fixed((rows, width)),
            fixed((rows, width)),
            fixed((8, width)),
            pl.BlockSpec((1, 4, width // 4, FF_BLOCK), lambda j: (j, 0, 0, 0)),
            pl.BlockSpec((8, 1, 1, cut, FF_BLOCK), lambda j: (0, j // 2, j % 2, 0, 0)),
            pl.BlockSpec((1, FF_BLOCK), lambda j: (0, j)),
        ),
        out_shape=(
            jax.ShapeDtypeStruct((rows, width), BF16),
            jax.ShapeDtypeStruct((rows, width), F32),
            jax.ShapeDtypeStruct((rows, width), BF16),
            jax.ShapeDtypeStruct((rows, width), BF16),
            jax.ShapeDtypeStruct((8, width), F32),
            jax.ShapeDtypeStruct((8, 4, width // 4, FF_BLOCK), BF16),
            jax.ShapeDtypeStruct((8, 4, 2, cut, FF_BLOCK), BF16),
            jax.ShapeDtypeStruct((1, hidden), F32),
        ),
        scratch_shapes=[
            pltpu.VMEM((rows, width), F32),
            pltpu.VMEM((rows, width), F32),
            pltpu.VMEM((rows, 1), F32),
            pltpu.VMEM((rows, width), F32),
            pltpu.VMEM((rows, width), BF16),
            pltpu.VMEM((rows, width), BF16),
            pltpu.VMEM((rows, width), F32),
            pltpu.VMEM((rows, width), F32),
        ],
        cost_estimate=pl.CostEstimate(
            flops=12 * rows * width * hidden, bytes_accessed=32 * 1024 * 1024, transcendentals=0
        ),
        name="mlp_both",
    )(attended, tokens, cotangent, out_weight, vectors, up_weight, up_bias, down_weight)


def grads_kernel(
    dq0, dq1, own0, own1, fl0, fl1, fr0, fr1, normed, gattn, attended,
    gproj, one, two, sums, acc, wt, og,
):
    rows, width = dq0.shape
    for m, (dq, own, left, right) in enumerate(
        ((dq0, own0, fl0, fr0), (dq1, own1, fl1, fr1))
    ):
        acc[...] = own[...]
        acc[0:HALO, :] += left[...].astype(F32)
        acc[rows - HALO :, :] += right[...].astype(F32)
        gproj[m * rows : (m + 1) * rows, 0:width] = dq[...]
        gproj[m * rows : (m + 1) * rows, width:] = acc[...].astype(BF16)
    og[...] = dot_tn(gattn[...], attended[...])
    cols = 3 * width // 8
    cut = width // 8
    half = (cols + cut) // 2
    lane = lax.broadcasted_iota(jnp.int32, (half, 2 * (width // 4)), 1)
    first = lane < width // 4
    for k in range(2):
        part = gproj[:, 4 * cols * k : 4 * cols * (k + 1)]
        sums[:, 4 * cols * k : 4 * cols * (k + 1)] = column_sum(part.astype(F32))
        wt[...] = dot_tn(part, normed[...])
        for tt in range(4):
            t = 4 * k + tt
            for x in range(2):
                span = slice(2 * (width // 4) * x, 2 * (width // 4) * (x + 1))
                top = wt[cols * tt : cols * tt + half, span]
                bottom = jnp.concatenate(
                    [wt[cols * tt + half : cols * (tt + 1), span], og[cut * t : cut * (t + 1), span]],
                    axis=0,
                )
                even = jnp.where(first, top, pltpu.roll(bottom, width // 4, 1)).astype(BF16)
                odd = jnp.where(first, pltpu.roll(top, width // 4, 1), bottom).astype(BF16)
                one[t, 2 * x] = even[: half // 2]
                two[t, 2 * x] = even[half // 2 :]
                one[t, 2 * x + 1] = odd[: half // 2]
                two[t, 2 * x + 1] = odd[half // 2 :]


def grads_call(*operands):
    rows, width = operands[0].shape
    total = operands[8].shape[0]
    shape = (8, 4, width // 8, width // 2)
    return pl.pallas_call(
        grads_kernel,
        in_specs=[vmem()] * 11,
        out_specs=(vmem(),) * 4,
        out_shape=(
            jax.ShapeDtypeStruct((total, 3 * width), BF16),
            jax.ShapeDtypeStruct(shape, BF16),
            jax.ShapeDtypeStruct(shape, BF16),
            jax.ShapeDtypeStruct((1, 3 * width), F32),
        ),
        scratch_shapes=[
            pltpu.VMEM((rows, 2 * width), F32),
            pltpu.VMEM((3 * width // 2, width), F32),
            pltpu.VMEM((width, width), F32),
        ],
        cost_estimate=pl.CostEstimate(
            flops=8 * total * width * width, bytes_accessed=24 * 1024 * 1024, transcendentals=0
        ),
        name="qkv_grads",
    )(*operands)


def shift_right(values, size):
    return lax.ppermute(values, "head", [(i, i + 1) for i in range(size - 1)])


def shift_left(values, size):
    return lax.ppermute(values, "head", [(i + 1, i) for i in range(size - 1)])


def axis_bits(size):
    return size.bit_length() - 1


def bit_orders(tok_size, head_size):
    tok = [("tok", b) for b in range(axis_bits(tok_size))]
    head = [("head", b) for b in range(axis_bits(head_size))]
    return head + tok, head[:1] + tok + head[1:]


def swap_pairs(size, bit):
    return [(i, i ^ (1 << bit)) for i in range(size)]


class BlockSum:
    def __init__(self, blocks, order, sizes):
        self.dims = [("tok", b) for b in reversed(range(axis_bits(sizes["tok"])))]
        self.dims += [("head", b) for b in reversed(range(axis_bits(sizes["head"])))]
        self.part = blocks.reshape((2,) * len(self.dims) + blocks.shape[2:])
        self.order = list(order)
        self.sizes = sizes
        self.flight = None

    def cut(self):
        self.step = self.order.pop(0)
        axis, bit = self.step
        where = self.dims.index(self.step)
        mine = (lax.axis_index(axis) >> bit) & 1
        send = lax.dynamic_index_in_dim(self.part, 1 - mine, where, keepdims=False)
        self.keep = lax.dynamic_index_in_dim(self.part, mine, where, keepdims=False)
        self.dims.pop(where)
        return [send]

    def send(self, parts):
        axis, bit = self.step
        return [lax.ppermute(parts[0], axis, swap_pairs(self.sizes[axis], bit))]

    def join(self, got):
        part = self.keep.astype(F32) + got[0].astype(F32)
        self.part = part.astype(BF16) if self.order else part


class SmallSum:
    def __init__(self, values, sizes):
        self.part = values
        self.sizes = sizes
        self.order = []
        for axis in ("head", "tok"):
            bits = axis_bits(sizes[axis])
            self.order += [(axis, b, min(2, bits - b)) for b in range(0, bits, 2)]

    def cut(self):
        self.step = self.order.pop(0)
        return [self.part]

    def send(self, parts):
        axis, bit, count = self.step
        size = self.sizes[axis]
        masks = [1 << bit] if count == 1 else [1 << bit, 2 << bit, 3 << bit]
        return [lax.ppermute(parts[0], axis, [(i, i ^ m) for i in range(size)]) for m in masks]

    def join(self, got):
        part = self.part + got[0]
        self.part = part + (got[1] + got[2]) if len(got) > 1 else part


def launch(sums, *tied):
    pieces = [s.cut() for s in sums]
    flat, tied = lax.optimization_barrier((pieces, tied))
    flights = [s.send(p) for s, p in zip(sums, flat)]
    return flights, tied


def land(sums, flights):
    flights = lax.optimization_barrier(flights)
    for s, got in zip(sums, flights):
        s.join(got)


def per_device(
    sizes,
    tokens,
    crop_start,
    crop_len,
    attn_gain,
    attn_shift,
    qkv_weight,
    query_bias,
    value_bias,
    out_weight,
    out_bias,
    attn_scale,
    mlp_gain,
    mlp_shift,
    up_weight,
    up_bias,
    down_weight,
    down_bias,
    mlp_scale,
    cotangent,
):
    micro, rows, width = tokens.shape
    hidden = up_weight.shape[1]
    tok_size, head_size = sizes["tok"], sizes["head"]
    window = rows + 2 * HALO
    head_at = lax.axis_index("head")
    order_a, order_b = bit_orders(tok_size, head_size)
    kv_bias = jnp.concatenate([jnp.zeros_like(value_bias), value_bias])
    qkv_bias = jnp.concatenate([query_bias, kv_bias])

    halo_left = shift_right(tokens[:, rows - HALO :, :], head_size)
    halo_right = shift_left(tokens[:, :HALO, :], head_size)

    total_rows = micro * rows
    inputs_f = tokens.reshape(total_rows, width).astype(F32)
    normal_one, inv_one = norm_stats(inputs_f)
    normed_low = (normal_one * attn_gain + attn_shift).astype(BF16)
    qkv = (dot_nn(normed_low, qkv_weight) + qkv_bias).astype(BF16)

    halo = jnp.stack([halo_left, halo_right]).reshape(2 * micro * HALO, width)
    halo_normal, _ = norm_stats(halo.astype(F32))
    halo_low = (halo_normal * attn_gain + attn_shift).astype(BF16)
    halo_kv = (dot_nn(halo_low, qkv_weight[:, width:]) + kv_bias).astype(BF16)
    halo_kv = halo_kv.reshape(2, micro, HALO, 2 * width)

    bounds = []
    attended_parts = []
    for m in range(micro):
        low, high = crop_bounds(
            crop_start[m, 0], crop_len[m, 0], head_at * rows, rows, head_size * rows
        )
        ranges = tile_ranges(low, high, window)
        bounds.append((ranges, low[:, None], high[:, None]))
        own = qkv[m * rows : (m + 1) * rows]
        attended_parts.append(attention_forward(*bounds[m], halo_kv[0, m], own, halo_kv[1, m]))
    attended = jnp.concatenate(attended_parts, axis=0)

    vectors = jnp.stack(
        [
            out_bias,
            attn_scale,
            mlp_gain,
            mlp_shift,
            mlp_scale,
            down_bias,
            jnp.zeros_like(out_bias),
            jnp.zeros_like(out_bias),
        ]
    )
    output, grad_mid, grad_attn, grad_attended, small, up_blocks, down_blocks, sum_up_bias = mlp_call(
        attended,
        tokens.reshape(total_rows, width),
        cotangent.reshape(total_rows, width),
        out_weight,
        vectors,
        up_weight,
        up_bias[None, :],
        down_weight,
    )
    more = tok_size // 8
    if more > 1:
        up_blocks = up_blocks.reshape(8, 4, width // 4, more, -1).transpose(0, 3, 1, 2, 4)
        up_blocks = up_blocks.reshape((tok_size,) + up_blocks.shape[2:])
        down_blocks = down_blocks.reshape(8, 4, 2, more, -1, FF_BLOCK).transpose(0, 3, 1, 2, 4, 5)
        down_blocks = down_blocks.reshape((tok_size,) + down_blocks.shape[2:])
    up_sum = BlockSum(up_blocks, order_b, sizes)
    down_sum = BlockSum(down_blocks, order_a, sizes)

    grads = []
    early = [up_sum, down_sum]
    for m in range(micro):
        grad = grad_attended[m * rows : (m + 1) * rows]
        flights, (grad,) = launch(early, grad)
        own = qkv[m * rows : (m + 1) * rows]
        dq, dleft, dkv, dright = attention_backward(
            *bounds[m], halo_kv[0, m], own, halo_kv[1, m], grad
        )
        halos = (shift_right(dright, head_size), shift_left(dleft, head_size))
        grads.append((dq, dkv) + halos)
        if m + 1 < micro:
            land(early, flights)
    (dq0, own0, fl0, fr0), (dq1, own1, fl1, fr1) = grads
    land(early, flights)
    flights, (dq1,) = launch(early, dq1)
    grad_projected, one, two, sum_qkv_bias = grads_call(
        dq0, dq1, own0, own1, fl0, fl1, fr0, fr1, normed_low, grad_attn, attended
    )
    if more > 1:
        whole = jnp.concatenate([one, two], axis=2)
        tall = jnp.concatenate(jnp.split(whole, 2, axis=3), axis=2)
        cols = 3 * width // 8
        pieces = [tall[:, :, :cols], tall[:, :, cols:]]
        pieces = [p.reshape(8, 4, more, -1, width // 4).transpose(0, 2, 1, 3, 4) for p in pieces]
        tall = jnp.concatenate(pieces, axis=3)
        tall = tall.reshape((tok_size,) + tall.shape[2:])
        half = tall.shape[2] // 2
        one, two = tall[:, :, :half], tall[:, :, half:]
    late = [BlockSum(one, order_a, sizes), BlockSum(two, order_b, sizes)]
    flying, (grad_projected,) = launch(late, grad_projected)
    land(early, flights)

    grad_normed_one = dot_nt(grad_projected, qkv_weight)
    grad_norm_one, sum_attn_gain, sum_attn_shift = norm_backward(
        grad_normed_one, attn_gain, normal_one, inv_one
    )
    input_grad = grad_mid + grad_norm_one
    w = width
    sum_qkv_bias = sum_qkv_bias.reshape(-1)
    vecs = jnp.concatenate(
        [
            small[:6].reshape(-1),
            sum_up_bias.reshape(-1),
            sum_attn_gain,
            sum_attn_shift,
            sum_qkv_bias[:w],
            sum_qkv_bias[2 * w :],
        ]
    ).reshape(-1, LANES)
    vecs = SmallSum(vecs, sizes)
    land(late, flying)
    everything = late + early + [vecs]
    while any(s.order for s in everything):
        active = [s for s in everything if s.order]
        flights, _ = launch(active)
        land(active, flights)
    one, two, up, down = [s.part for s in late + early]
    vecs = vecs.part.reshape(-1)
    tall = jnp.concatenate([one, two], axis=0)
    if more == 1:
        tall = jnp.concatenate(jnp.split(tall, 2, axis=1), axis=0)
    grad_qkv = tall[: 3 * width // tok_size].T
    grad_out = tall[3 * width // tok_size :].T
    grad_up_weight = up
    grad_down = down.transpose(0, 2, 1).reshape(hidden // head_size, width // tok_size)
    early = vecs[: 6 * w].reshape(6, w)
    late = vecs[6 * w + hidden :].reshape(4, w)
    return (
        output.reshape(micro, rows, width),
        input_grad.reshape(micro, rows, width),
        late[0],
        late[1],
        grad_qkv,
        late[2],
        late[3],
        grad_out,
        early[0],
        early[1],
        early[2],
        early[3],
        grad_up_weight,
        vecs[6 * w : 6 * w + hidden],
        grad_down,
        early[4],
        early[5],
    )


def solution(mesh):
    sizes = {"tok": mesh.shape["tok"], "head": mesh.shape["head"]}
    rows = P(None, ("tok", "head"), None)
    crops = P(None, "tok", None)
    whole = P()
    split = P("head", "tok")
    return jax.shard_map(
        partial(per_device, sizes),
        mesh=mesh,
        in_specs=(rows, crops, crops) + (whole,) * 15 + (rows,),
        out_specs=(
            rows,
            rows,
            whole,
            whole,
            split,
            whole,
            whole,
            split,
            whole,
            whole,
            whole,
            whole,
            split,
            whole,
            split,
            whole,
            whole,
        ),
        check_vma=False,
    )
```

```python
import jax
import jax.numpy as jnp
from jax import lax
from jax.experimental import pallas as pl
from jax.experimental.pallas import tpu as pltpu
from jax.sharding import PartitionSpec as P

HEAD_DIM = 64
NORM_EPS = 1e-06
MASKED = -1e30
HALO = 272
QT = 128
LANES = 128
FF_BLOCK = 384
UNROLL = 6
TILE_COUNTS = (2, 3, 4, 6)
F32 = jnp.float32
BF16 = jnp.bfloat16


def norm_stats(values):
    center = jnp.mean(values, axis=-1, keepdims=True)
    centered = values - center
    variance = jnp.mean(centered * centered, axis=-1, keepdims=True)
    inv_std = lax.rsqrt(variance + NORM_EPS)
    return centered * inv_std, inv_std


def norm_backward(grad_out, gain, normal_rows, inv_std):
    scaled = grad_out * gain
    mean_one = jnp.mean(scaled, axis=-1, keepdims=True)
    mean_two = jnp.mean(scaled * normal_rows, axis=-1, keepdims=True)
    grad_in = inv_std * (scaled - mean_one - normal_rows * mean_two)
    return grad_in, jnp.sum(grad_out * normal_rows, axis=0), jnp.sum(grad_out, axis=0)


def dot_nn(a, b):
    return lax.dot_general(a, b, (((1,), (0,)), ((), ())), preferred_element_type=F32)


def dot_nt(a, b):
    return lax.dot_general(a, b, (((1,), (1,)), ((), ())), preferred_element_type=F32)


def dot_tn(a, b):
    return lax.dot_general(a, b, (((0,), (0,)), ((), ())), preferred_element_type=F32)


def crop_bounds(starts, lengths, first_row, rows, group_rows):
    row_ids = first_row + lax.iota(jnp.int32, rows)[:, None]
    ends = jnp.minimum(starts + lengths, group_rows)
    inside = (row_ids >= starts[None, :]) & (row_ids < ends[None, :])
    found = jnp.any(inside, axis=1)
    low = jnp.where(found, jnp.sum(jnp.where(inside, starts[None, :], 0), axis=1), row_ids[:, 0])
    high = jnp.where(found, jnp.sum(jnp.where(inside, ends[None, :], 0), axis=1), row_ids[:, 0] + 1)
    return low - first_row + HALO, high - first_row + HALO


def tile_ranges(low, high, window):
    tiles = low.shape[0] // QT
    first = (low.reshape(tiles, QT)[:, 0] // 16) * 16
    last = high.reshape(tiles, QT)[:, QT - 1]
    need = (last - first + LANES - 1) // LANES
    count = jnp.full_like(need, TILE_COUNTS[-1])
    for n in reversed(TILE_COUNTS[:-1]):
        count = jnp.where(need <= n, n, count)
    first = jnp.clip(first, 0, window - count * LANES)
    return jnp.concatenate([first, count]).astype(jnp.int32)


def load_window(left, own, right, win, width):
    rows = own.shape[0]
    win[0:HALO, :] = left[...]
    win[HALO : HALO + rows, :] = own[:, width:]
    win[HALO + rows :, :] = right[...]


def pair_stack(values):
    lane = lax.broadcasted_iota(jnp.int32, values.shape, 1)
    zero = jnp.zeros_like(values)
    one = jnp.where(lane < HEAD_DIM, values, zero)
    two = jnp.where(lane < HEAD_DIM, zero, values)
    return jnp.concatenate([one, two], axis=0)


def pair_merge(values):
    both = jnp.concatenate([values[:HEAD_DIM, :QT], values[HEAD_DIM:, QT:]], axis=0)
    return both.T


def tile_bias(low_ref, high_ref, row0, first, span):
    key_at = first + lax.broadcasted_iota(jnp.int32, (span, QT), 0)
    low = low_ref[:, pl.ds(row0, QT)]
    high = high_ref[:, pl.ds(row0, QT)]
    same = (key_at >= low) & (key_at < high)
    bias = jnp.where(same, 0.0, MASKED).astype(F32)
    return jnp.concatenate([bias, bias], axis=1)


def forward_kernel(ranges, low_ref, high_ref, left, own, right, out, log_sums, win):
    width = out.shape[1]
    rows = own.shape[0]
    tiles = rows // QT
    load_window(left, own, right, win, width)

    def tile(i, carry):
        row0 = pl.multiple_of(i * QT, QT)
        first = pl.multiple_of(ranges[i], 16)
        count = ranges[tiles + i]
        for n in TILE_COUNTS:

            @pl.when(count == n)
            def _():
                span = n * LANES
                bias = tile_bias(low_ref, high_ref, row0, first, span)

                def pair(p, inner):
                    col = pl.multiple_of(p * LANES, LANES)
                    vcol = pl.multiple_of(width + p * LANES, LANES)
                    query = own[pl.ds(row0, QT), pl.ds(col, LANES)]
                    stacked = pair_stack(query * jnp.asarray(0.125, BF16))
                    keys = win[pl.ds(first, span), pl.ds(col, LANES)]
                    scores = dot_nt(keys, stacked) + bias
                    peak = jnp.max(scores, axis=0, keepdims=True)
                    expo = jnp.exp(scores - peak)
                    total = jnp.sum(expo, axis=0, keepdims=True)
                    vals = win[pl.ds(first, span), pl.ds(vcol, LANES)]
                    res = dot_tn(vals, expo.astype(BF16)) / total
                    out[pl.ds(row0, QT), pl.ds(col, LANES)] = pair_merge(res).astype(BF16)
                    at = pl.multiple_of(2 * row0, 2 * QT)
                    log_sums[pl.ds(p, 1), pl.ds(at, 2 * QT)] = peak + jnp.log(total)
                    return inner

                lax.fori_loop(0, width // LANES, pair, 0, unroll=UNROLL)

        return carry

    lax.fori_loop(0, tiles, tile, 0)


def backward_kernel(
    ranges, low_ref, high_ref, left, own, right, log_sums, grad, dq, dleft, down, dright, win, acc
):
    width = grad.shape[1]
    rows = own.shape[0]
    tiles = rows // QT
    load_window(left, own, right, win, width)
    acc[...] = jnp.zeros_like(acc)

    def tile(i, carry):
        row0 = pl.multiple_of(i * QT, QT)
        first = pl.multiple_of(ranges[i], 16)
        count = ranges[tiles + i]
        for n in TILE_COUNTS:

            @pl.when(count == n)
            def _():
                span = n * LANES
                bias = tile_bias(low_ref, high_ref, row0, first, span)

                def pair(p, inner):
                    col = pl.multiple_of(p * LANES, LANES)
                    vcol = pl.multiple_of(width + p * LANES, LANES)
                    query = own[pl.ds(row0, QT), pl.ds(col, LANES)]
                    stacked = pair_stack(query * jnp.asarray(0.125, BF16))
                    gstack = pair_stack(grad[pl.ds(row0, QT), pl.ds(col, LANES)])
                    keys = win[pl.ds(first, span), pl.ds(col, LANES)]
                    vals = win[pl.ds(first, span), pl.ds(vcol, LANES)]
                    at = pl.multiple_of(2 * row0, 2 * QT)
                    lse = log_sums[pl.ds(p, 1), pl.ds(at, 2 * QT)]
                    probs = jnp.exp(dot_nt(keys, stacked) + bias - lse)
                    dprobs = dot_nt(vals, gstack)
                    row_dot = jnp.sum(probs * dprobs, axis=0, keepdims=True)
                    dscores = (probs * (dprobs - row_dot)).astype(BF16)
                    res = dot_tn(keys, dscores) * 0.125
                    dq[pl.ds(row0, QT), pl.ds(col, LANES)] = pair_merge(res).astype(BF16)
                    acc[pl.ds(first, span), pl.ds(col, LANES)] += dot_nn(dscores, stacked)
                    acc[pl.ds(first, span), pl.ds(vcol, LANES)] += dot_nn(
                        probs.astype(BF16), gstack
                    )
                    return inner

                lax.fori_loop(0, width // LANES, pair, 0, unroll=UNROLL)

        return carry

    lax.fori_loop(0, tiles, tile, 0)
    dleft[...] = acc[0:HALO, :].astype(BF16)
    down[...] = acc[HALO : HALO + rows, :]
    dright[...] = acc[HALO + rows :, :].astype(BF16)


def smem():
    return pl.BlockSpec(memory_space=pltpu.SMEM)


def vmem():
    return pl.BlockSpec(memory_space=pltpu.VMEM)


def attention_forward(ranges, low, high, left, own, right):
    rows, width = own.shape[0], own.shape[1] // 3
    window = rows + 2 * HALO
    return pl.pallas_call(
        forward_kernel,
        out_shape=(
            jax.ShapeDtypeStruct((rows, width), BF16),
            jax.ShapeDtypeStruct((8, 2 * rows), F32),
        ),
        in_specs=[smem()] + [vmem()] * 5,
        out_specs=(vmem(), vmem()),
        scratch_shapes=[pltpu.VMEM((window, 2 * width), BF16)],
        cost_estimate=pl.CostEstimate(
            flops=4 * rows * 640 * width * 4, bytes_accessed=8 * 1024 * 1024, transcendentals=0
        ),
        name="attn_fwd",
    )(ranges, low, high, left, own, right)


def attention_backward(ranges, low, high, left, own, right, log_sums, grad):
    rows, width = grad.shape
    window = rows + 2 * HALO
    return pl.pallas_call(
        backward_kernel,
        out_shape=(
            jax.ShapeDtypeStruct((rows, width), BF16),
            jax.ShapeDtypeStruct((HALO, 2 * width), BF16),
            jax.ShapeDtypeStruct((rows, 2 * width), F32),
            jax.ShapeDtypeStruct((HALO, 2 * width), BF16),
        ),
        in_specs=[smem()] + [vmem()] * 7,
        out_specs=(vmem(),) * 4,
        scratch_shapes=[
            pltpu.VMEM((window, 2 * width), BF16),
            pltpu.VMEM((window, 2 * width), F32),
        ],
        cost_estimate=pl.CostEstimate(
            flops=10 * rows * 640 * width * 4, bytes_accessed=16 * 1024 * 1024, transcendentals=0
        ),
        name="attn_bwd",
    )(ranges, low, high, left, own, right, log_sums, grad)


def column_sum(values):
    return jnp.sum(values, axis=0, keepdims=True)


def mlp_kernel(
    attended,
    tokens,
    cotangent,
    out_weight,
    vectors,
    up_weight,
    up_bias,
    down_weight,
    output,
    grad_mid,
    grad_attn,
    grad_attended,
    small,
    up_grad,
    down_grad,
    up_bias_grad,
    mid,
    normal,
    inv_std,
    branch,
    low,
    grad_mlp,
    acc,
    err,
):
    step = pl.program_id(0)
    out_bias, attn_scale = vectors[0:1, :], vectors[1:2, :]
    gain, shift = vectors[2:3, :], vectors[3:4, :]
    mlp_scale, down_bias = vectors[4:5, :], vectors[5:6, :]

    @pl.when(step == 0)
    def _():
        first = dot_nn(attended[...], out_weight[...]) + out_bias
        branch[...] = first
        total = tokens[...].astype(F32) + attn_scale * first
        mid[...] = total
        rows_n, inv = norm_stats(total)
        normal[...] = rows_n
        inv_std[...] = inv
        low[...] = (rows_n * gain + shift).astype(BF16)
        grad_mlp[...] = (mlp_scale * cotangent[...].astype(F32)).astype(BF16)
        acc[...] = jnp.zeros_like(acc)
        err[...] = jnp.zeros_like(err)

    up_pre = dot_nn(low[...], up_weight[...]) + up_bias[...]
    cdf = 0.5 * (1.0 + lax.erf(up_pre * 0.7071067811865476))
    slope = cdf + up_pre * (0.3989422804014327 * jnp.exp(-0.5 * up_pre * up_pre))
    active = (up_pre * cdf).astype(BF16)
    grad_up = (slope * dot_nt(grad_mlp[...], down_weight[...])).astype(BF16)
    acc[...] += dot_nn(active, down_weight[...])
    err[...] += dot_nt(grad_up, up_weight[...])
    up_bias_grad[...] = column_sum(grad_up.astype(F32))
    up_grad[...] = dot_tn(low[...], grad_up).astype(BF16).reshape(up_grad.shape)
    down_grad[...] = dot_tn(grad_mlp[...], active).astype(BF16).reshape(down_grad.shape)

    @pl.when(step == pl.num_programs(0) - 1)
    def _():
        grad_out = cotangent[...].astype(F32)
        mlp_branch = acc[...] + down_bias
        output[...] = (mid[...] + mlp_scale * mlp_branch).astype(BF16)
        e = err[...]
        rows_n = normal[...]
        scaled = e * gain
        mean_one = jnp.mean(scaled, axis=-1, keepdims=True)
        mean_two = jnp.mean(scaled * rows_n, axis=-1, keepdims=True)
        total = grad_out + inv_std[...] * (scaled - mean_one - rows_n * mean_two)
        grad_mid[...] = total
        low_grad = (attn_scale * total).astype(BF16)
        grad_attn[...] = low_grad
        grad_attended[...] = dot_nt(low_grad, out_weight[...]).astype(BF16)
        small[0:1, :] = column_sum(low_grad.astype(F32))
        small[1:2, :] = column_sum(total * branch[...])
        small[2:3, :] = column_sum(e * rows_n)
        small[3:4, :] = column_sum(e)
        small[4:5, :] = column_sum(grad_mlp[...].astype(F32))
        small[5:6, :] = column_sum(grad_out * mlp_branch)
        small[6:8, :] = jnp.zeros((2, small.shape[1]), F32)


def mlp_call(attended, tokens, cotangent, out_weight, vectors, up_weight, up_bias, down_weight):
    rows, width = tokens.shape
    hidden = up_weight.shape[1]
    steps = hidden // FF_BLOCK
    cut = width // 8
    fixed = lambda shape: pl.BlockSpec(shape, lambda j: (0,) * len(shape))
    return pl.pallas_call(
        mlp_kernel,
        grid=(steps,),
        in_specs=[
            fixed((rows, width)),
            fixed((rows, width)),
            fixed((rows, width)),
            fixed((width, width)),
            fixed((8, width)),
            pl.BlockSpec((width, FF_BLOCK), lambda j: (0, j)),
            pl.BlockSpec((1, FF_BLOCK), lambda j: (0, j)),
            pl.BlockSpec((FF_BLOCK, width), lambda j: (j, 0)),
        ],
        out_specs=(
            fixed((rows, width)),
            fixed((rows, width)),
            fixed((rows, width)),
            fixed((rows, width)),
            fixed((8, width)),
            pl.BlockSpec((1, 4, width // 4, FF_BLOCK), lambda j: (j, 0, 0, 0)),
            pl.BlockSpec((8, 1, 1, cut, FF_BLOCK), lambda j: (0, j // 2, j % 2, 0, 0)),
            pl.BlockSpec((1, FF_BLOCK), lambda j: (0, j)),
        ),
        out_shape=(
            jax.ShapeDtypeStruct((rows, width), BF16),
            jax.ShapeDtypeStruct((rows, width), F32),
            jax.ShapeDtypeStruct((rows, width), BF16),
            jax.ShapeDtypeStruct((rows, width), BF16),
            jax.ShapeDtypeStruct((8, width), F32),
            jax.ShapeDtypeStruct((8, 4, width // 4, FF_BLOCK), BF16),
            jax.ShapeDtypeStruct((8, 4, 2, cut, FF_BLOCK), BF16),
            jax.ShapeDtypeStruct((1, hidden), F32),
        ),
        scratch_shapes=[
            pltpu.VMEM((rows, width), F32),
            pltpu.VMEM((rows, width), F32),
            pltpu.VMEM((rows, 1), F32),
            pltpu.VMEM((rows, width), F32),
            pltpu.VMEM((rows, width), BF16),
            pltpu.VMEM((rows, width), BF16),
            pltpu.VMEM((rows, width), F32),
            pltpu.VMEM((rows, width), F32),
        ],
        cost_estimate=pl.CostEstimate(
            flops=12 * rows * width * hidden, bytes_accessed=32 * 1024 * 1024, transcendentals=0
        ),
        name="mlp_both",
    )(attended, tokens, cotangent, out_weight, vectors, up_weight, up_bias, down_weight)


def grads_kernel(
    dq0, dq1, own0, own1, fl0, fl1, fr0, fr1, normed, gattn, attended,
    gproj, one, two, sums, acc, wt, og,
):
    rows, width = dq0.shape
    for m, (dq, own, left, right) in enumerate(
        ((dq0, own0, fl0, fr0), (dq1, own1, fl1, fr1))
    ):
        acc[...] = own[...]
        acc[0:HALO, :] += left[...].astype(F32)
        acc[rows - HALO :, :] += right[...].astype(F32)
        gproj[m * rows : (m + 1) * rows, 0:width] = dq[...]
        gproj[m * rows : (m + 1) * rows, width:] = acc[...].astype(BF16)
    og[...] = dot_tn(gattn[...], attended[...])
    cols = 3 * width // 8
    cut = width // 8
    half = (cols + cut) // 2
    lane = lax.broadcasted_iota(jnp.int32, (half, 2 * (width // 4)), 1)
    first = lane < width // 4
    for k in range(2):
        part = gproj[:, 4 * cols * k : 4 * cols * (k + 1)]
        sums[:, 4 * cols * k : 4 * cols * (k + 1)] = column_sum(part.astype(F32))
        wt[...] = dot_tn(part, normed[...])
        for tt in range(4):
            t = 4 * k + tt
            for x in range(2):
                span = slice(2 * (width // 4) * x, 2 * (width // 4) * (x + 1))
                top = wt[cols * tt : cols * tt + half, span]
                bottom = jnp.concatenate(
                    [wt[cols * tt + half : cols * (tt + 1), span], og[cut * t : cut * (t + 1), span]],
                    axis=0,
                )
                even = jnp.where(first, top, pltpu.roll(bottom, width // 4, 1)).astype(BF16)
                odd = jnp.where(first, pltpu.roll(top, width // 4, 1), bottom).astype(BF16)
                one[t, 2 * x] = even[: half // 2]
                two[t, 2 * x] = even[half // 2 :]
                one[t, 2 * x + 1] = odd[: half // 2]
                two[t, 2 * x + 1] = odd[half // 2 :]


def grads_call(*operands):
    rows, width = operands[0].shape
    total = operands[8].shape[0]
    shape = (8, 4, width // 8, width // 2)
    return pl.pallas_call(
        grads_kernel,
        in_specs=[vmem()] * 11,
        out_specs=(vmem(),) * 4,
        out_shape=(
            jax.ShapeDtypeStruct((total, 3 * width), BF16),
            jax.ShapeDtypeStruct(shape, BF16),
            jax.ShapeDtypeStruct(shape, BF16),
            jax.ShapeDtypeStruct((1, 3 * width), F32),
        ),
        scratch_shapes=[
            pltpu.VMEM((rows, 2 * width), F32),
            pltpu.VMEM((3 * width // 2, width), F32),
            pltpu.VMEM((width, width), F32),
        ],
        cost_estimate=pl.CostEstimate(
            flops=8 * total * width * width, bytes_accessed=24 * 1024 * 1024, transcendentals=0
        ),
        name="qkv_grads",
    )(*operands)


def shift_right(values, size):
    return lax.ppermute(values, "head", [(i, i + 1) for i in range(size - 1)])


def shift_left(values, size):
    return lax.ppermute(values, "head", [(i + 1, i) for i in range(size - 1)])


def axis_bits(size):
    return size.bit_length() - 1


def bit_orders(tok_size, head_size):
    tok = [("tok", b) for b in range(axis_bits(tok_size))]
    head = [("head", b) for b in range(axis_bits(head_size))]
    return head + tok, head[:1] + tok + head[1:]


def swap_pairs(size, bit):
    return [(i, i ^ (1 << bit)) for i in range(size)]


class BlockSum:
    def __init__(self, blocks, order, sizes):
        self.dims = [("tok", b) for b in reversed(range(axis_bits(sizes["tok"])))]
        self.dims += [("head", b) for b in reversed(range(axis_bits(sizes["head"])))]
        self.part = blocks.reshape((2,) * len(self.dims) + blocks.shape[2:])
        self.order = list(order)
        self.sizes = sizes

    def cut(self):
        self.step = self.order.pop(0)
        axis, bit = self.step
        where = self.dims.index(self.step)
        mine = (lax.axis_index(axis) >> bit) & 1
        send = lax.dynamic_index_in_dim(self.part, 1 - mine, where, keepdims=False)
        self.keep = lax.dynamic_index_in_dim(self.part, mine, where, keepdims=False)
        self.dims.pop(where)
        return [send]

    def send(self, parts):
        axis, bit = self.step
        return [lax.ppermute(parts[0], axis, swap_pairs(self.sizes[axis], bit))]

    def join(self, got):
        part = self.keep.astype(F32) + got[0].astype(F32)
        self.part = part.astype(BF16) if self.order else part


class SmallSum:
    def __init__(self, values, sizes):
        self.part = values
        self.sizes = sizes
        self.order = []
        for axis in ("head", "tok"):
            bits = axis_bits(sizes[axis])
            self.order += [(axis, b, min(2, bits - b)) for b in range(0, bits, 2)]

    def cut(self):
        self.step = self.order.pop(0)
        return [self.part]

    def send(self, parts):
        axis, bit, count = self.step
        size = self.sizes[axis]
        masks = [1 << bit] if count == 1 else [1 << bit, 2 << bit, 3 << bit]
        return [lax.ppermute(parts[0], axis, [(i, i ^ m) for i in range(size)]) for m in masks]

    def join(self, got):
        part = self.part + got[0]
        self.part = part + (got[1] + got[2]) if len(got) > 1 else part


def launch(sums, *tied):
    pieces = [s.cut() for s in sums]
    flat, tied = lax.optimization_barrier((pieces, tied))
    flights = []
    for s, p in zip(sums, flat):
        flights.append(s.send(p))
    return flights, tied


def land(sums, flights, *tied):
    flights, tied = lax.optimization_barrier((flights, tied))
    for s, got in zip(sums, flights):
        s.join(got)
    return tied


def per_device(
    sizes,
    tokens,
    crop_start,
    crop_len,
    attn_gain,
    attn_shift,
    qkv_weight,
    query_bias,
    value_bias,
    out_weight,
    out_bias,
    attn_scale,
    mlp_gain,
    mlp_shift,
    up_weight,
    up_bias,
    down_weight,
    down_bias,
    mlp_scale,
    cotangent,
):
    micro, rows, width = tokens.shape
    hidden = up_weight.shape[1]
    tok_size, head_size = sizes["tok"], sizes["head"]
    window = rows + 2 * HALO
    head_at = lax.axis_index("head")
    order_a, order_b = bit_orders(tok_size, head_size)
    kv_bias = jnp.concatenate([jnp.zeros_like(value_bias), value_bias])
    qkv_bias = jnp.concatenate([query_bias, kv_bias])

    halo_left = shift_right(tokens[:, rows - HALO :, :], head_size)
    halo_right = shift_left(tokens[:, :HALO, :], head_size)

    total_rows = micro * rows
    inputs_f = tokens.reshape(total_rows, width).astype(F32)
    normal_one, inv_one = norm_stats(inputs_f)
    normed_low = (normal_one * attn_gain + attn_shift).astype(BF16)
    qkv = (dot_nn(normed_low, qkv_weight) + qkv_bias).astype(BF16)

    halo = jnp.stack([halo_left, halo_right]).reshape(2 * micro * HALO, width)
    halo_normal, _ = norm_stats(halo.astype(F32))
    halo_low = (halo_normal * attn_gain + attn_shift).astype(BF16)
    halo_kv = (dot_nn(halo_low, qkv_weight[:, width:]) + kv_bias).astype(BF16)
    halo_kv = halo_kv.reshape(2, micro, HALO, 2 * width)

    bounds = []
    attended_parts, log_sums = [], []
    for m in range(micro):
        low, high = crop_bounds(
            crop_start[m, 0], crop_len[m, 0], head_at * rows, rows, head_size * rows
        )
        ranges = tile_ranges(low, high, window)
        bounds.append((ranges, low[None, :], high[None, :]))
        own = qkv[m * rows : (m + 1) * rows]
        part, sums = attention_forward(*bounds[m], halo_kv[0, m], own, halo_kv[1, m])
        attended_parts.append(part)
        log_sums.append(sums)
    attended = jnp.concatenate(attended_parts, axis=0)

    vectors = jnp.stack(
        [
            out_bias,
            attn_scale,
            mlp_gain,
            mlp_shift,
            mlp_scale,
            down_bias,
            jnp.zeros_like(out_bias),
            jnp.zeros_like(out_bias),
        ]
    )
    output, grad_mid, grad_attn, grad_attended, small, up_blocks, down_blocks, sum_up_bias = mlp_call(
        attended,
        tokens.reshape(total_rows, width),
        cotangent.reshape(total_rows, width),
        out_weight,
        vectors,
        up_weight,
        up_bias[None, :],
        down_weight,
    )
    more = tok_size // 8
    if more > 1:
        up_blocks = up_blocks.reshape(8, 4, width // 4, more, -1).transpose(0, 3, 1, 2, 4)
        up_blocks = up_blocks.reshape((tok_size,) + up_blocks.shape[2:])
        down_blocks = down_blocks.reshape(8, 4, 2, more, -1, FF_BLOCK).transpose(0, 3, 1, 2, 4, 5)
        down_blocks = down_blocks.reshape((tok_size,) + down_blocks.shape[2:])
    up_sum = BlockSum(up_blocks, order_b, sizes)
    down_sum = BlockSum(down_blocks, order_a, sizes)

    grads = []
    early = [up_sum, down_sum]
    for m in range(micro):
        grad = grad_attended[m * rows : (m + 1) * rows]
        flights, (grad,) = launch(early, grad)
        own = qkv[m * rows : (m + 1) * rows]
        dq, dleft, dkv, dright = attention_backward(
            *bounds[m], halo_kv[0, m], own, halo_kv[1, m], log_sums[m], grad
        )
        from_left = shift_right(dright, head_size)
        from_right = shift_left(dleft, head_size)
        (dq,) = land(early, flights, dq)
        grads.append((dq, dkv, from_left, from_right))
    (dq0, own0, fl0, fr0), (dq1, own1, fl1, fr1) = grads
    flights, (dq1,) = launch(early, dq1)
    grad_projected, one, two, sum_qkv_bias = grads_call(
        dq0, dq1, own0, own1, fl0, fl1, fr0, fr1, normed_low, grad_attn, attended
    )
    if more > 1:
        whole = jnp.concatenate([one, two], axis=2)
        tall = jnp.concatenate(jnp.split(whole, 2, axis=3), axis=2)
        cols = 3 * width // 8
        pieces = [tall[:, :, :cols], tall[:, :, cols:]]
        pieces = [p.reshape(8, 4, more, -1, width // 4).transpose(0, 2, 1, 3, 4) for p in pieces]
        tall = jnp.concatenate(pieces, axis=3)
        tall = tall.reshape((tok_size,) + tall.shape[2:])
        half = tall.shape[2] // 2
        one, two = tall[:, :, :half], tall[:, :, half:]
    late = [BlockSum(one, order_a, sizes), BlockSum(two, order_b, sizes)]
    flying, (grad_projected,) = launch(late, grad_projected)

    grad_normed_one = dot_nt(grad_projected, qkv_weight)
    grad_norm_one, sum_attn_gain, sum_attn_shift = norm_backward(
        grad_normed_one, attn_gain, normal_one, inv_one
    )
    input_grad = grad_mid + grad_norm_one
    land(early, flights)
    w = width
    sum_qkv_bias = sum_qkv_bias.reshape(-1)
    vecs = jnp.concatenate(
        [
            small[:6].reshape(-1),
            sum_up_bias.reshape(-1),
            sum_attn_gain,
            sum_attn_shift,
            sum_qkv_bias[:w],
            sum_qkv_bias[2 * w :],
        ]
    ).reshape(-1, LANES)
    vecs = SmallSum(vecs, sizes)
    land(late, flying)
    everything = late + early + [vecs]
    while any(s.order for s in everything):
        active = [s for s in everything if s.order]
        flights, _ = launch(active)
        land(active, flights)
    one, two, up, down = [s.part for s in late + early]
    vecs = vecs.part.reshape(-1)
    tall = jnp.concatenate([one, two], axis=0)
    if more == 1:
        tall = jnp.concatenate(jnp.split(tall, 2, axis=1), axis=0)
    grad_qkv = tall[: 3 * width // tok_size].T
    grad_out = tall[3 * width // tok_size :].T
    grad_up_weight = up
    grad_down = down.transpose(0, 2, 1).reshape(hidden // head_size, width // tok_size)
    early = vecs[: 6 * w].reshape(6, w)
    late = vecs[6 * w + hidden :].reshape(4, w)
    return (
        output.reshape(micro, rows, width),
        input_grad.reshape(micro, rows, width),
        late[0],
        late[1],
        grad_qkv,
        late[2],
        late[3],
        grad_out,
        early[0],
        early[1],
        early[2],
        early[3],
        grad_up_weight,
        vecs[6 * w : 6 * w + hidden],
        grad_down,
        early[4],
        early[5],
    )


def solution(mesh):
    sizes = {"tok": mesh.shape["tok"], "head": mesh.shape["head"]}
    rows = P(None, ("tok", "head"), None)
    crops = P(None, "tok", None)
    whole = P()
    split = P("head", "tok")

    def body(*args):
        return per_device(sizes, *args)

    return jax.shard_map(
        body,
        mesh=mesh,
        in_specs=(rows, crops, crops) + (whole,) * 15 + (rows,),
        out_specs=(
            rows,
            rows,
            whole,
            whole,
            split,
            whole,
            whole,
            split,
            whole,
            whole,
            whole,
            whole,
            split,
            whole,
            split,
            whole,
            whole,
        ),
        check_vma=False,
    )
```

```python
import jax
import jax.numpy as jnp
from jax import lax
from jax.experimental import pallas as pl
from jax.experimental.pallas import tpu as pltpu
from jax.sharding import PartitionSpec as P

HEAD_DIM = 64
NORM_EPS = 1e-06
MASKED = -1e30
HALO = 272
QT = 128
LANES = 128
FF_BLOCK = 384
UNROLL = 6
TILE_COUNTS = (2, 3, 4, 6)
F32 = jnp.float32
BF16 = jnp.bfloat16


def norm_stats(values):
    center = jnp.mean(values, axis=-1, keepdims=True)
    centered = values - center
    variance = jnp.mean(centered * centered, axis=-1, keepdims=True)
    inv_std = lax.rsqrt(variance + NORM_EPS)
    return centered * inv_std, inv_std


def dot_nn(a, b):
    return lax.dot_general(a, b, (((1,), (0,)), ((), ())), preferred_element_type=F32)


def dot_nt(a, b):
    return lax.dot_general(a, b, (((1,), (1,)), ((), ())), preferred_element_type=F32)


def dot_tn(a, b):
    return lax.dot_general(a, b, (((0,), (0,)), ((), ())), preferred_element_type=F32)


def crop_bounds(starts, lengths, first_row, rows, group_rows):
    row_ids = first_row + lax.iota(jnp.int32, rows)[:, None]
    ends = jnp.minimum(starts + lengths, group_rows)
    inside = (row_ids >= starts[None, :]) & (row_ids < ends[None, :])
    found = jnp.any(inside, axis=1)
    low = jnp.where(found, jnp.sum(jnp.where(inside, starts[None, :], 0), axis=1), row_ids[:, 0])
    high = jnp.where(found, jnp.sum(jnp.where(inside, ends[None, :], 0), axis=1), row_ids[:, 0] + 1)
    return low - first_row + HALO, high - first_row + HALO


def tile_ranges(low, high, window):
    tiles = low.shape[0] // QT
    first = (low.reshape(tiles, QT)[:, 0] // 16) * 16
    last = high.reshape(tiles, QT)[:, QT - 1]
    need = (last - first + LANES - 1) // LANES
    count = jnp.full_like(need, TILE_COUNTS[-1])
    for n in reversed(TILE_COUNTS[:-1]):
        count = jnp.where(need <= n, n, count)
    first = jnp.clip(first, 0, window - count * LANES)
    return jnp.concatenate([first, count]).astype(jnp.int32)


def load_window(left, own, right, win, width):
    rows = own.shape[0]
    win[0:HALO, :] = left[...]
    win[HALO : HALO + rows, :] = own[:, width:]
    win[HALO + rows :, :] = right[...]


def pair_stack(values):
    lane = lax.broadcasted_iota(jnp.int32, values.shape, 1)
    zero = jnp.zeros_like(values)
    one = jnp.where(lane < HEAD_DIM, values, zero)
    two = jnp.where(lane < HEAD_DIM, zero, values)
    return jnp.concatenate([one, two], axis=0)


def pair_merge(values):
    both = jnp.concatenate([values[:HEAD_DIM, :QT], values[HEAD_DIM:, QT:]], axis=0)
    return both.T


def tile_bias(low_ref, high_ref, row0, first, span):
    key_at = first + lax.broadcasted_iota(jnp.int32, (span, QT), 0)
    low = low_ref[:, pl.ds(row0, QT)]
    high = high_ref[:, pl.ds(row0, QT)]
    same = (key_at >= low) & (key_at < high)
    bias = jnp.where(same, 0.0, MASKED).astype(F32)
    return jnp.concatenate([bias, bias], axis=1)


def forward_kernel(ranges, low_ref, high_ref, left, own, right, out, log_sums, win):
    width = out.shape[1]
    rows = own.shape[0]
    tiles = rows // QT
    load_window(left, own, right, win, width)

    def tile(i, carry):
        row0 = pl.multiple_of(i * QT, QT)
        first = pl.multiple_of(ranges[i], 16)
        count = ranges[tiles + i]
        for n in TILE_COUNTS:

            @pl.when(count == n)
            def _():
                span = n * LANES
                bias = tile_bias(low_ref, high_ref, row0, first, span)

                def pair(p, inner):
                    col = pl.multiple_of(p * LANES, LANES)
                    vcol = pl.multiple_of(width + p * LANES, LANES)
                    query = own[pl.ds(row0, QT), pl.ds(col, LANES)]
                    stacked = pair_stack(query * jnp.asarray(0.125, BF16))
                    keys = win[pl.ds(first, span), pl.ds(col, LANES)]
                    scores = dot_nt(keys, stacked) + bias
                    peak = jnp.max(scores, axis=0, keepdims=True)
                    expo = jnp.exp(scores - peak)
                    total = jnp.sum(expo, axis=0, keepdims=True)
                    vals = win[pl.ds(first, span), pl.ds(vcol, LANES)]
                    res = dot_tn(vals, expo.astype(BF16)) / total
                    out[pl.ds(row0, QT), pl.ds(col, LANES)] = pair_merge(res).astype(BF16)
                    at = pl.multiple_of(2 * row0, 2 * QT)
                    log_sums[pl.ds(p, 1), pl.ds(at, 2 * QT)] = peak + jnp.log(total)
                    return inner

                lax.fori_loop(0, width // LANES, pair, 0, unroll=UNROLL)

        return carry

    lax.fori_loop(0, tiles, tile, 0)


def backward_kernel(
    ranges, low_ref, high_ref, left, own, right, log_sums, grad, dq, dleft, down, dright, win, acc
):
    width = grad.shape[1]
    rows = own.shape[0]
    tiles = rows // QT
    load_window(left, own, right, win, width)
    acc[...] = jnp.zeros_like(acc)

    def tile(i, carry):
        row0 = pl.multiple_of(i * QT, QT)
        first = pl.multiple_of(ranges[i], 16)
        count = ranges[tiles + i]
        for n in TILE_COUNTS:

            @pl.when(count == n)
            def _():
                span = n * LANES
                bias = tile_bias(low_ref, high_ref, row0, first, span)

                def pair(p, inner):
                    col = pl.multiple_of(p * LANES, LANES)
                    vcol = pl.multiple_of(width + p * LANES, LANES)
                    query = own[pl.ds(row0, QT), pl.ds(col, LANES)]
                    stacked = pair_stack(query * jnp.asarray(0.125, BF16))
                    gstack = pair_stack(grad[pl.ds(row0, QT), pl.ds(col, LANES)])
                    keys = win[pl.ds(first, span), pl.ds(col, LANES)]
                    vals = win[pl.ds(first, span), pl.ds(vcol, LANES)]
                    at = pl.multiple_of(2 * row0, 2 * QT)
                    lse = log_sums[pl.ds(p, 1), pl.ds(at, 2 * QT)]
                    probs = jnp.exp(dot_nt(keys, stacked) + bias - lse)
                    dprobs = dot_nt(vals, gstack)
                    row_dot = jnp.sum(probs * dprobs, axis=0, keepdims=True)
                    dscores = (probs * (dprobs - row_dot)).astype(BF16)
                    res = dot_tn(keys, dscores) * 0.125
                    dq[pl.ds(row0, QT), pl.ds(col, LANES)] = pair_merge(res).astype(BF16)
                    acc[pl.ds(first, span), pl.ds(col, LANES)] += dot_nn(dscores, stacked)
                    acc[pl.ds(first, span), pl.ds(vcol, LANES)] += dot_nn(
                        probs.astype(BF16), gstack
                    )
                    return inner

                lax.fori_loop(0, width // LANES, pair, 0, unroll=UNROLL)

        return carry

    lax.fori_loop(0, tiles, tile, 0)
    dleft[...] = acc[0:HALO, :].astype(BF16)
    down[...] = acc[HALO : HALO + rows, :]
    dright[...] = acc[HALO + rows :, :].astype(BF16)


def smem():
    return pl.BlockSpec(memory_space=pltpu.SMEM)


def vmem():
    return pl.BlockSpec(memory_space=pltpu.VMEM)


def attention_forward(ranges, low, high, left, own, right):
    rows, width = own.shape[0], own.shape[1] // 3
    window = rows + 2 * HALO
    return pl.pallas_call(
        forward_kernel,
        out_shape=(
            jax.ShapeDtypeStruct((rows, width), BF16),
            jax.ShapeDtypeStruct((8, 2 * rows), F32),
        ),
        in_specs=[smem()] + [vmem()] * 5,
        out_specs=(vmem(), vmem()),
        scratch_shapes=[pltpu.VMEM((window, 2 * width), BF16)],
        cost_estimate=pl.CostEstimate(
            flops=4 * rows * 640 * width * 4, bytes_accessed=8 * 1024 * 1024, transcendentals=0
        ),
        name="attn_fwd",
    )(ranges, low, high, left, own, right)


def attention_backward(ranges, low, high, left, own, right, log_sums, grad):
    rows, width = grad.shape
    window = rows + 2 * HALO
    return pl.pallas_call(
        backward_kernel,
        out_shape=(
            jax.ShapeDtypeStruct((rows, width), BF16),
            jax.ShapeDtypeStruct((HALO, 2 * width), BF16),
            jax.ShapeDtypeStruct((rows, 2 * width), F32),
            jax.ShapeDtypeStruct((HALO, 2 * width), BF16),
        ),
        in_specs=[smem()] + [vmem()] * 7,
        out_specs=(vmem(),) * 4,
        scratch_shapes=[
            pltpu.VMEM((window, 2 * width), BF16),
            pltpu.VMEM((window, 2 * width), F32),
        ],
        cost_estimate=pl.CostEstimate(
            flops=10 * rows * 640 * width * 4, bytes_accessed=16 * 1024 * 1024, transcendentals=0
        ),
        name="attn_bwd",
    )(ranges, low, high, left, own, right, log_sums, grad)


def column_sum(values):
    return jnp.sum(values, axis=0, keepdims=True)


def mlp_kernel(
    core,
    attended,
    tokens,
    cotangent,
    out_weight,
    vectors,
    up_weight,
    up_bias,
    down_weight,
    output,
    grad_mid,
    grad_attn,
    grad_attended,
    small,
    up_keep,
    up_send,
    down_keep,
    down_send,
    up_bias_grad,
    mid,
    normal,
    inv_std,
    branch,
    low,
    grad_mlp,
    acc,
    err,
):
    step = pl.program_id(0)
    out_bias, attn_scale = vectors[0:1, :], vectors[1:2, :]
    gain, shift = vectors[2:3, :], vectors[3:4, :]
    mlp_scale, down_bias = vectors[4:5, :], vectors[5:6, :]

    @pl.when(step == 0)
    def _():
        first = dot_nn(attended[...], out_weight[...]) + out_bias
        branch[...] = first
        total = tokens[...].astype(F32) + attn_scale * first
        mid[...] = total
        rows_n, inv = norm_stats(total)
        normal[...] = rows_n
        inv_std[...] = inv
        low[...] = (rows_n * gain + shift).astype(BF16)
        grad_mlp[...] = (mlp_scale * cotangent[...].astype(F32)).astype(BF16)
        acc[...] = jnp.zeros_like(acc)
        err[...] = jnp.zeros_like(err)

    up_pre = dot_nn(low[...], up_weight[...]) + up_bias[...]
    cdf = 0.5 * (1.0 + lax.erf(up_pre * 0.7071067811865476))
    slope = cdf + up_pre * (0.3989422804014327 * jnp.exp(-0.5 * up_pre * up_pre))
    active = (up_pre * cdf).astype(BF16)
    grad_up = (slope * dot_nt(grad_mlp[...], down_weight[...])).astype(BF16)
    acc[...] += dot_nn(active, down_weight[...])
    err[...] += dot_nt(grad_up, up_weight[...])
    up_bias_grad[0] = column_sum(grad_up.astype(F32))
    mine = core[0]
    up_grad = dot_tn(low[...], grad_up).astype(BF16)
    up_grad = up_grad.reshape(2, 2, up_keep.shape[2], up_keep.shape[3])
    for c in range(2):

        @pl.when(mine == c)
        def _():
            up_keep[0] = up_grad[:, c]
            up_send[0] = up_grad[:, 1 - c]

    down_grad = dot_tn(grad_mlp[...], active).astype(BF16)
    down_grad = down_grad.reshape(down_keep.shape[0], down_keep.shape[3], down_keep.shape[4])

    @pl.when((step // 2) % 2 == mine)
    def _():
        down_keep[:, step // 4, step % 2] = down_grad

    @pl.when((step // 2) % 2 != mine)
    def _():
        down_send[:, step // 4, step % 2] = down_grad

    @pl.when(step == pl.num_programs(0) - 1)
    def _():
        grad_out = cotangent[...].astype(F32)
        mlp_branch = acc[...] + down_bias
        output[...] = (mid[...] + mlp_scale * mlp_branch).astype(BF16)
        e = err[...]
        rows_n = normal[...]
        scaled = e * gain
        mean_one = jnp.mean(scaled, axis=-1, keepdims=True)
        mean_two = jnp.mean(scaled * rows_n, axis=-1, keepdims=True)
        total = grad_out + inv_std[...] * (scaled - mean_one - rows_n * mean_two)
        grad_mid[...] = total
        low_grad = (attn_scale * total).astype(BF16)
        grad_attn[...] = low_grad
        grad_attended[...] = dot_nt(low_grad, out_weight[...]).astype(BF16)
        small[0:1, :] = column_sum(low_grad.astype(F32))
        small[1:2, :] = column_sum(total * branch[...])
        small[2:3, :] = column_sum(e * rows_n)
        small[3:4, :] = column_sum(e)
        small[4:5, :] = column_sum(grad_mlp[...].astype(F32))
        small[5:6, :] = column_sum(grad_out * mlp_branch)
        small[6:8, :] = jnp.zeros((2, small.shape[1]), F32)


def mlp_call(core, attended, tokens, cotangent, out_weight, vectors, up_weight, up_bias, down_weight):
    rows, width = tokens.shape
    hidden = up_weight.shape[1]
    steps = hidden // FF_BLOCK
    cut = width // 8
    fixed = lambda shape: pl.BlockSpec(shape, lambda j: (0,) * len(shape))
    return pl.pallas_call(
        mlp_kernel,
        grid=(steps,),
        in_specs=[
            smem(),
            fixed((rows, width)),
            fixed((rows, width)),
            fixed((rows, width)),
            fixed((width, width)),
            fixed((8, width)),
            pl.BlockSpec((width, FF_BLOCK), lambda j: (0, j)),
            pl.BlockSpec((1, FF_BLOCK), lambda j: (0, j)),
            pl.BlockSpec((FF_BLOCK, width), lambda j: (j, 0)),
        ],
        out_specs=(
            fixed((rows, width)),
            fixed((rows, width)),
            fixed((rows, width)),
            fixed((rows, width)),
            fixed((8, width)),
            pl.BlockSpec((1, 2, width // 4, FF_BLOCK), lambda j: (j, 0, 0, 0)),
            pl.BlockSpec((1, 2, width // 4, FF_BLOCK), lambda j: (j, 0, 0, 0)),
            fixed((8, 2, 2, cut, FF_BLOCK)),
            fixed((8, 2, 2, cut, FF_BLOCK)),
            pl.BlockSpec((1, 1, FF_BLOCK), lambda j: (j // 2, 0, j % 2)),
        ),
        out_shape=(
            jax.ShapeDtypeStruct((rows, width), BF16),
            jax.ShapeDtypeStruct((rows, width), F32),
            jax.ShapeDtypeStruct((rows, width), BF16),
            jax.ShapeDtypeStruct((rows, width), BF16),
            jax.ShapeDtypeStruct((8, width), F32),
            jax.ShapeDtypeStruct((8, 2, width // 4, FF_BLOCK), BF16),
            jax.ShapeDtypeStruct((8, 2, width // 4, FF_BLOCK), BF16),
            jax.ShapeDtypeStruct((8, 2, 2, cut, FF_BLOCK), BF16),
            jax.ShapeDtypeStruct((8, 2, 2, cut, FF_BLOCK), BF16),
            jax.ShapeDtypeStruct((hidden // width, 1, width), F32),
        ),
        scratch_shapes=[
            pltpu.VMEM((rows, width), F32),
            pltpu.VMEM((rows, width), F32),
            pltpu.VMEM((rows, 1), F32),
            pltpu.VMEM((rows, width), F32),
            pltpu.VMEM((rows, width), BF16),
            pltpu.VMEM((rows, width), BF16),
            pltpu.VMEM((rows, width), F32),
            pltpu.VMEM((rows, width), F32),
        ],
        cost_estimate=pl.CostEstimate(
            flops=12 * rows * width * hidden, bytes_accessed=32 * 1024 * 1024, transcendentals=0
        ),
        name="mlp_both",
    )(core, attended, tokens, cotangent, out_weight, vectors, up_weight, up_bias, down_weight)


def grads_kernel(
    core, dq0, dq1, own0, own1, fl0, fl1, fr0, fr1, normed, gattn, attended,
    gproj, one_keep, one_send, two_keep, two_send, sums, acc, wt, og,
):
    rows, width = dq0.shape
    for m, (dq, own, left, right) in enumerate(
        ((dq0, own0, fl0, fr0), (dq1, own1, fl1, fr1))
    ):
        acc[...] = own[...]
        acc[0:HALO, :] += left[...].astype(F32)
        acc[rows - HALO :, :] += right[...].astype(F32)
        gproj[m * rows : (m + 1) * rows, 0:width] = dq[...]
        gproj[m * rows : (m + 1) * rows, width:] = acc[...].astype(BF16)
    og[...] = dot_tn(gattn[...], attended[...])
    cols = 3 * width // 8
    cut = width // 8
    half = (cols + cut) // 2
    lane = lax.broadcasted_iota(jnp.int32, (half, 2 * (width // 4)), 1)
    first = lane < width // 4
    for k in range(2):
        part = gproj[:, 4 * cols * k : 4 * cols * (k + 1)]
        sums[:, 4 * cols * k : 4 * cols * (k + 1)] = column_sum(part.astype(F32))
        wt[...] = dot_tn(part, normed[...])
        for tt in range(4):
            t = 4 * k + tt
            for x in range(2):
                span = slice(2 * (width // 4) * x, 2 * (width // 4) * (x + 1))
                top = wt[cols * tt : cols * tt + half, span]
                bottom = jnp.concatenate(
                    [wt[cols * tt + half : cols * (tt + 1), span], og[cut * t : cut * (t + 1), span]],
                    axis=0,
                )
                even = jnp.where(first, top, pltpu.roll(bottom, width // 4, 1)).astype(BF16)
                odd = jnp.where(first, pltpu.roll(top, width // 4, 1), bottom).astype(BF16)
                for c, (keep, send) in enumerate(((even, odd), (odd, even))):

                    @pl.when(core[0] == c)
                    def _():
                        one_keep[t, x] = keep[: half // 2]
                        two_keep[t, x] = keep[half // 2 :]
                        one_send[t, x] = send[: half // 2]
                        two_send[t, x] = send[half // 2 :]


def grads_call(*operands):
    rows, width = operands[1].shape
    total = operands[9].shape[0]
    shape = (8, 2, width // 8, width // 2)
    return pl.pallas_call(
        grads_kernel,
        in_specs=[smem()] + [vmem()] * 11,
        out_specs=(vmem(),) * 6,
        out_shape=(
            jax.ShapeDtypeStruct((total, 3 * width), BF16),
            jax.ShapeDtypeStruct(shape, BF16),
            jax.ShapeDtypeStruct(shape, BF16),
            jax.ShapeDtypeStruct(shape, BF16),
            jax.ShapeDtypeStruct(shape, BF16),
            jax.ShapeDtypeStruct((1, 3 * width), F32),
        ),
        scratch_shapes=[
            pltpu.VMEM((rows, 2 * width), F32),
            pltpu.VMEM((3 * width // 2, width), F32),
            pltpu.VMEM((width, width), F32),
        ],
        cost_estimate=pl.CostEstimate(
            flops=8 * total * width * width, bytes_accessed=24 * 1024 * 1024, transcendentals=0
        ),
        name="qkv_grads",
    )(*operands)


def inner_kernel(
    grad_proj, weight, tokens, grad_mid, gain, small, up_bias_sum, qkv_sums, input_grad, vecs
):
    width = tokens.shape[1]

    @pl.when(pl.program_id(0) == 0)
    def _():
        vecs[0:6, :] = small[0:6, :]
        for k in range(4):
            vecs[6 + k : 7 + k, :] = up_bias_sum[k]
        vecs[10:16, :] = jnp.zeros((6, width), F32)
        vecs[12:13, :] = qkv_sums[:, 0:width]
        vecs[13:14, :] = qkv_sums[:, 2 * width :]

    f = dot_nt(grad_proj[...], weight[...])
    rows_n, inv = norm_stats(tokens[...].astype(F32))
    scaled = f * gain[...]
    mean_one = jnp.mean(scaled, axis=-1, keepdims=True)
    mean_two = jnp.mean(scaled * rows_n, axis=-1, keepdims=True)
    input_grad[...] = grad_mid[...] + inv * (scaled - mean_one - rows_n * mean_two)
    vecs[10:11, :] += column_sum(f * rows_n)
    vecs[11:12, :] += column_sum(f)


def inner_call(grad_proj, weight, tokens, grad_mid, gain, small, up_bias_sum, qkv_sums):
    total, width = tokens.shape
    block = total // 3
    fixed = lambda shape: pl.BlockSpec(shape, lambda j: (0,) * len(shape))
    return pl.pallas_call(
        inner_kernel,
        grid=(3,),
        in_specs=[
            pl.BlockSpec((block, 3 * width), lambda j: (j, 0)),
            fixed((width, 3 * width)),
            pl.BlockSpec((block, width), lambda j: (j, 0)),
            pl.BlockSpec((block, width), lambda j: (j, 0)),
            fixed((1, width)),
            fixed((8, width)),
            fixed((4, 1, width)),
            fixed((1, 3 * width)),
        ],
        out_specs=(pl.BlockSpec((block, width), lambda j: (j, 0)), fixed((16, width))),
        out_shape=(
            jax.ShapeDtypeStruct((total, width), F32),
            jax.ShapeDtypeStruct((16, width), F32),
        ),
        cost_estimate=pl.CostEstimate(
            flops=6 * total * width * width, bytes_accessed=14 * 1024 * 1024, transcendentals=0
        ),
        name="inner",
    )(grad_proj, weight, tokens, grad_mid, gain, small, up_bias_sum, qkv_sums)


def shift_right(values, size):
    return lax.ppermute(values, "head", [(i, i + 1) for i in range(size - 1)])


def shift_left(values, size):
    return lax.ppermute(values, "head", [(i + 1, i) for i in range(size - 1)])


def axis_bits(size):
    return size.bit_length() - 1


def bit_orders(tok_size, head_size):
    tok = [("tok", b) for b in range(axis_bits(tok_size))]
    head = [("head", b) for b in range(axis_bits(head_size))]
    return head + tok, head[:1] + tok + head[1:]


def swap_pairs(size, bit):
    return [(i, i ^ (1 << bit)) for i in range(size)]


class BlockSum:
    def __init__(self, keep, send, order, sizes):
        self.dims = [("tok", b) for b in reversed(range(axis_bits(sizes["tok"])))]
        self.dims += [("head", b) for b in reversed(range(axis_bits(sizes["head"])))]
        self.dims.remove(order[0])
        self.keep = keep.reshape((2,) * len(self.dims) + keep.shape[2:])
        self.first = send.reshape(self.keep.shape)
        self.order = list(order)
        self.sizes = sizes

    def cut(self):
        self.step = self.order.pop(0)
        if self.step not in self.dims:
            return [self.first]
        axis, bit = self.step
        where = self.dims.index(self.step)
        mine = (lax.axis_index(axis) >> bit) & 1
        send = lax.dynamic_index_in_dim(self.part, 1 - mine, where, keepdims=False)
        self.keep = lax.dynamic_index_in_dim(self.part, mine, where, keepdims=False)
        self.dims.pop(where)
        return [send]

    def send(self, parts):
        axis, bit = self.step
        return [lax.ppermute(parts[0], axis, swap_pairs(self.sizes[axis], bit))]

    def join(self, got):
        part = self.keep.astype(F32) + got[0].astype(F32)
        self.part = part.astype(BF16) if self.order else part


class SmallSum:
    def __init__(self, values, sizes):
        self.part = values
        self.sizes = sizes
        self.order = []
        for axis in ("head", "tok"):
            bits = axis_bits(sizes[axis])
            self.order += [(axis, b, min(2, bits - b)) for b in range(0, bits, 2)]

    def cut(self):
        self.step = self.order.pop(0)
        return [self.part]

    def send(self, parts):
        axis, bit, count = self.step
        size = self.sizes[axis]
        masks = [1 << bit] if count == 1 else [1 << bit, 2 << bit, 3 << bit]
        return [lax.ppermute(parts[0], axis, [(i, i ^ m) for i in range(size)]) for m in masks]

    def join(self, got):
        part = self.part + got[0]
        self.part = part + (got[1] + got[2]) if len(got) > 1 else part


def launch(sums, *tied):
    pieces = [s.cut() for s in sums]
    flat, tied = lax.optimization_barrier((pieces, tied))
    flights = []
    for s, p in zip(sums, flat):
        flights.append(s.send(p))
    return flights, tied


def land(sums, flights, *tied):
    flights, tied = lax.optimization_barrier((flights, tied))
    for s, got in zip(sums, flights):
        s.join(got)
    return tied


def regroup_up(blocks, more):
    lead, head, rows, cols = blocks.shape
    blocks = blocks.reshape(lead, head, rows, more, cols // more).transpose(0, 3, 1, 2, 4)
    return blocks.reshape(lead * more, head, rows, cols // more)


def regroup_down(blocks, more):
    lead, head, half, rows, cols = blocks.shape
    blocks = blocks.reshape(lead, head, half, more, rows // more, cols)
    return blocks.transpose(0, 3, 1, 2, 4, 5).reshape(lead * more, head, half, rows // more, cols)


def regroup_qkv(one, two, more):
    tall = jnp.concatenate([one, two], axis=2)
    tall = jnp.concatenate(jnp.split(tall, 2, axis=3), axis=2)
    lead, head, rows, cols = tall.shape
    cut = 3 * rows // 4
    pieces = [tall[:, :, :cut], tall[:, :, cut:]]
    pieces = [p.reshape(lead, head, more, -1, cols).transpose(0, 2, 1, 3, 4) for p in pieces]
    tall = jnp.concatenate(pieces, axis=3).reshape(lead * more, head, rows // more, cols)
    return tuple(jnp.split(tall, 2, axis=2))


def per_device(
    sizes,
    tokens,
    crop_start,
    crop_len,
    attn_gain,
    attn_shift,
    qkv_weight,
    query_bias,
    value_bias,
    out_weight,
    out_bias,
    attn_scale,
    mlp_gain,
    mlp_shift,
    up_weight,
    up_bias,
    down_weight,
    down_bias,
    mlp_scale,
    cotangent,
):
    micro, rows, width = tokens.shape
    hidden = up_weight.shape[1]
    tok_size, head_size = sizes["tok"], sizes["head"]
    window = rows + 2 * HALO
    head_at = lax.axis_index("head")
    order_a, order_b = bit_orders(tok_size, head_size)
    kv_bias = jnp.concatenate([jnp.zeros_like(value_bias), value_bias])
    qkv_bias = jnp.concatenate([query_bias, kv_bias])

    halo_left = shift_right(tokens[:, rows - HALO :, :], head_size)
    halo_right = shift_left(tokens[:, :HALO, :], head_size)

    total_rows = micro * rows
    inputs_f = tokens.reshape(total_rows, width).astype(F32)
    normal_one, _ = norm_stats(inputs_f)
    normed_low = (normal_one * attn_gain + attn_shift).astype(BF16)
    qkv = (dot_nn(normed_low, qkv_weight) + qkv_bias).astype(BF16)

    halo = jnp.stack([halo_left, halo_right]).reshape(2 * micro * HALO, width)
    halo_normal, _ = norm_stats(halo.astype(F32))
    halo_low = (halo_normal * attn_gain + attn_shift).astype(BF16)
    halo_kv = (dot_nn(halo_low, qkv_weight[:, width:]) + kv_bias).astype(BF16)
    halo_kv = halo_kv.reshape(2, micro, HALO, 2 * width)

    bounds = []
    attended_parts, log_sums = [], []
    for m in range(micro):
        low, high = crop_bounds(
            crop_start[m, 0], crop_len[m, 0], head_at * rows, rows, head_size * rows
        )
        ranges = tile_ranges(low, high, window)
        bounds.append((ranges, low[None, :], high[None, :]))
        own = qkv[m * rows : (m + 1) * rows]
        part, sums = attention_forward(*bounds[m], halo_kv[0, m], own, halo_kv[1, m])
        attended_parts.append(part)
        log_sums.append(sums)
    attended = jnp.concatenate(attended_parts, axis=0)

    vectors = jnp.stack(
        [
            out_bias,
            attn_scale,
            mlp_gain,
            mlp_shift,
            mlp_scale,
            down_bias,
            jnp.zeros_like(out_bias),
            jnp.zeros_like(out_bias),
        ]
    )
    core = (head_at & 1).astype(jnp.int32).reshape(1)
    (
        output,
        grad_mid,
        grad_attn,
        grad_attended,
        small,
        up_keep,
        up_send,
        down_keep,
        down_send,
        up_bias_sum,
    ) = mlp_call(
        core,
        attended,
        tokens.reshape(total_rows, width),
        cotangent.reshape(total_rows, width),
        out_weight,
        vectors,
        up_weight,
        up_bias[None, :],
        down_weight,
    )
    more = tok_size // 8
    if more > 1:
        up_keep, up_send = regroup_up(up_keep, more), regroup_up(up_send, more)
        down_keep, down_send = regroup_down(down_keep, more), regroup_down(down_send, more)
    up_sum = BlockSum(up_keep, up_send, order_b, sizes)
    down_sum = BlockSum(down_keep, down_send, order_a, sizes)

    grads = []
    early = [up_sum, down_sum]
    for m in range(micro):
        grad = grad_attended[m * rows : (m + 1) * rows]
        flights, (grad,) = launch(early, grad)
        own = qkv[m * rows : (m + 1) * rows]
        dq, dleft, dkv, dright = attention_backward(
            *bounds[m], halo_kv[0, m], own, halo_kv[1, m], log_sums[m], grad
        )
        from_left = shift_right(dright, head_size)
        from_right = shift_left(dleft, head_size)
        (dq,) = land(early, flights, dq)
        grads.append((dq, dkv, from_left, from_right))
    (dq0, own0, fl0, fr0), (dq1, own1, fl1, fr1) = grads
    flights, (dq1,) = launch(early, dq1)
    grad_projected, one_keep, one_send, two_keep, two_send, qkv_sums = grads_call(
        core, dq0, dq1, own0, own1, fl0, fl1, fr0, fr1, normed_low, grad_attn, attended
    )
    if more > 1:
        one_keep, two_keep = regroup_qkv(one_keep, two_keep, more)
        one_send, two_send = regroup_qkv(one_send, two_send, more)
    late = [
        BlockSum(one_keep, one_send, order_a, sizes),
        BlockSum(two_keep, two_send, order_b, sizes),
    ]
    late_flights, _ = launch(late)
    land(early, flights)
    flights, _ = launch(early)
    land(late, late_flights)
    late_flights, (grad_projected,) = launch(late, grad_projected)
    land(early, flights)
    flights, _ = launch(early)
    input_grad, vecs = inner_call(
        grad_projected,
        qkv_weight,
        tokens.reshape(total_rows, width),
        grad_mid,
        attn_gain[None, :],
        small,
        up_bias_sum,
        qkv_sums,
    )
    (vecs,) = land(late, late_flights, vecs)
    land(early, flights)
    vecs = SmallSum(vecs, sizes)
    everything = late + early + [vecs]
    while any(s.order for s in everything):
        active = [s for s in everything if s.order]
        flights, _ = launch(active)
        land(active, flights)
    one, two, up, down = [s.part for s in late + early]
    vecs = vecs.part
    tall = jnp.concatenate([one, two], axis=0)
    if more == 1:
        tall = jnp.concatenate(jnp.split(tall, 2, axis=1), axis=0)
    grad_qkv = tall[: 3 * width // tok_size].T
    grad_out = tall[3 * width // tok_size :].T
    grad_up_weight = up
    grad_down = down.transpose(0, 2, 1).reshape(hidden // head_size, width // tok_size)
    early = vecs[:6]
    late = vecs[10:14]
    return (
        output.reshape(micro, rows, width),
        input_grad.reshape(micro, rows, width),
        late[0],
        late[1],
        grad_qkv,
        late[2],
        late[3],
        grad_out,
        early[0],
        early[1],
        early[2],
        early[3],
        grad_up_weight,
        vecs[6:10].reshape(hidden),
        grad_down,
        early[4],
        early[5],
    )


def solution(mesh):
    sizes = {"tok": mesh.shape["tok"], "head": mesh.shape["head"]}
    rows = P(None, ("tok", "head"), None)
    crops = P(None, "tok", None)
    whole = P()
    split = P("head", "tok")

    def body(*args):
        return per_device(sizes, *args)

    return jax.shard_map(
        body,
        mesh=mesh,
        in_specs=(rows, crops, crops) + (whole,) * 15 + (rows,),
        out_specs=(
            rows,
            rows,
            whole,
            whole,
            split,
            whole,
            whole,
            split,
            whole,
            whole,
            whole,
            whole,
            split,
            whole,
            split,
            whole,
            whole,
        ),
        check_vma=False,
    )
```

```python
from functools import partial

import jax
import jax.numpy as jnp
from jax import lax
from jax.experimental import pallas as pl
from jax.experimental.pallas import tpu as pltpu
from jax.sharding import PartitionSpec as P

HEAD_DIM = 64
NORM_EPS = 1e-06
MASKED = -1e30
HALO = 272
QT = 128
LANES = 128
FF_BLOCK = 384
UNROLL = 6
TILE_COUNTS = (2, 3, 4, 6)
F32 = jnp.float32
BF16 = jnp.bfloat16


def norm_stats(values):
    center = jnp.mean(values, axis=-1, keepdims=True)
    centered = values - center
    variance = jnp.mean(centered * centered, axis=-1, keepdims=True)
    inv_std = lax.rsqrt(variance + NORM_EPS)
    return centered * inv_std, inv_std


def dot_nn(a, b):
    return lax.dot_general(a, b, (((1,), (0,)), ((), ())), preferred_element_type=F32)


def dot_nt(a, b):
    return lax.dot_general(a, b, (((1,), (1,)), ((), ())), preferred_element_type=F32)


def dot_tn(a, b):
    return lax.dot_general(a, b, (((0,), (0,)), ((), ())), preferred_element_type=F32)


def crop_bounds(starts, lengths, first_row, rows, group_rows):
    row_ids = first_row + lax.iota(jnp.int32, rows)[:, None]
    ends = jnp.minimum(starts + lengths, group_rows)
    inside = (row_ids >= starts[None, :]) & (row_ids < ends[None, :])
    found = jnp.any(inside, axis=1)
    low = jnp.where(found, jnp.sum(jnp.where(inside, starts[None, :], 0), axis=1), row_ids[:, 0])
    high = jnp.where(found, jnp.sum(jnp.where(inside, ends[None, :], 0), axis=1), row_ids[:, 0] + 1)
    return low - first_row + HALO, high - first_row + HALO


def tile_ranges(low, high, window):
    tiles = low.shape[0] // QT
    first = (low.reshape(tiles, QT)[:, 0] // 16) * 16
    last = high.reshape(tiles, QT)[:, QT - 1]
    need = (last - first + LANES - 1) // LANES
    count = jnp.full_like(need, TILE_COUNTS[-1])
    for n in reversed(TILE_COUNTS[:-1]):
        count = jnp.where(need <= n, n, count)
    first = jnp.clip(first, 0, window - count * LANES)
    return jnp.concatenate([first, count]).astype(jnp.int32)


def load_window(left, own, right, win, width):
    rows = own.shape[0]
    win[0:HALO, :] = left[...]
    win[HALO : HALO + rows, :] = own[:, width:]
    win[HALO + rows :, :] = right[...]


def pair_stack(values):
    lane = lax.broadcasted_iota(jnp.int32, values.shape, 1)
    zero = jnp.zeros_like(values)
    one = jnp.where(lane < HEAD_DIM, values, zero)
    two = jnp.where(lane < HEAD_DIM, zero, values)
    return jnp.concatenate([one, two], axis=0)


def pair_merge(values):
    both = jnp.concatenate([values[:HEAD_DIM, :QT], values[HEAD_DIM:, QT:]], axis=0)
    return both.T


def tile_bias(low_ref, high_ref, row0, first, span):
    key_at = first + lax.broadcasted_iota(jnp.int32, (span, QT), 0)
    low = low_ref[:, pl.ds(row0, QT)]
    high = high_ref[:, pl.ds(row0, QT)]
    same = (key_at >= low) & (key_at < high)
    bias = jnp.where(same, 0.0, MASKED).astype(F32)
    return jnp.concatenate([bias, bias], axis=1)


def forward_kernel(ranges, low_ref, high_ref, left, own, right, out, log_sums, win):
    width = out.shape[1]
    rows = own.shape[0]
    tiles = rows // QT
    micro = pl.program_id(0)
    load_window(left, own, right, win, width)

    def tile(i, carry):
        row0 = pl.multiple_of(i * QT, QT)
        first = pl.multiple_of(ranges[micro, i], 16)
        count = ranges[micro, tiles + i]
        for n in TILE_COUNTS:

            @pl.when(count == n)
            def _():
                span = n * LANES
                bias = tile_bias(low_ref, high_ref, row0, first, span)

                def pair(p, inner):
                    col = pl.multiple_of(p * LANES, LANES)
                    vcol = pl.multiple_of(width + p * LANES, LANES)
                    query = own[pl.ds(row0, QT), pl.ds(col, LANES)]
                    stacked = pair_stack(query * jnp.asarray(0.125, BF16))
                    keys = win[pl.ds(first, span), pl.ds(col, LANES)]
                    scores = dot_nt(keys, stacked) + bias
                    peak = jnp.max(scores, axis=0, keepdims=True)
                    expo = jnp.exp(scores - peak)
                    total = jnp.sum(expo, axis=0, keepdims=True)
                    vals = win[pl.ds(first, span), pl.ds(vcol, LANES)]
                    res = dot_tn(vals, expo.astype(BF16)) / total
                    out[pl.ds(row0, QT), pl.ds(col, LANES)] = pair_merge(res).astype(BF16)
                    at = pl.multiple_of(2 * row0, 2 * QT)
                    log_sums[pl.ds(p, 1), pl.ds(at, 2 * QT)] = peak + jnp.log(total)
                    return inner

                lax.fori_loop(0, width // LANES, pair, 0, unroll=UNROLL)

        return carry

    lax.fori_loop(0, tiles, tile, 0)


def backward_kernel(
    micro, ranges, low_ref, high_ref, left, own, right, log_sums, grad, dq, dleft, down, dright, win, acc
):
    width = grad.shape[1]
    rows = own.shape[0]
    tiles = rows // QT
    load_window(left, own, right, win, width)
    acc[...] = jnp.zeros_like(acc)

    def tile(i, carry):
        row0 = pl.multiple_of(i * QT, QT)
        first = pl.multiple_of(ranges[micro, i], 16)
        count = ranges[micro, tiles + i]
        for n in TILE_COUNTS:

            @pl.when(count == n)
            def _():
                span = n * LANES
                bias = tile_bias(low_ref, high_ref, row0, first, span)

                def pair(p, inner):
                    col = pl.multiple_of(p * LANES, LANES)
                    vcol = pl.multiple_of(width + p * LANES, LANES)
                    query = own[pl.ds(row0, QT), pl.ds(col, LANES)]
                    stacked = pair_stack(query * jnp.asarray(0.125, BF16))
                    gstack = pair_stack(grad[pl.ds(row0, QT), pl.ds(col, LANES)])
                    keys = win[pl.ds(first, span), pl.ds(col, LANES)]
                    vals = win[pl.ds(first, span), pl.ds(vcol, LANES)]
                    at = pl.multiple_of(2 * row0, 2 * QT)
                    lse = log_sums[pl.ds(p, 1), pl.ds(at, 2 * QT)]
                    probs = jnp.exp(dot_nt(keys, stacked) + bias - lse)
                    dprobs = dot_nt(vals, gstack)
                    row_dot = jnp.sum(probs * dprobs, axis=0, keepdims=True)
                    dscores = (probs * (dprobs - row_dot)).astype(BF16)
                    res = dot_tn(keys, dscores) * 0.125
                    dq[pl.ds(row0, QT), pl.ds(col, LANES)] = pair_merge(res).astype(BF16)
                    acc[pl.ds(first, span), pl.ds(col, LANES)] += dot_nn(dscores, stacked)
                    acc[pl.ds(first, span), pl.ds(vcol, LANES)] += dot_nn(
                        probs.astype(BF16), gstack
                    )
                    return inner

                lax.fori_loop(0, width // LANES, pair, 0, unroll=UNROLL)

        return carry

    lax.fori_loop(0, tiles, tile, 0)
    dleft[...] = acc[0:HALO, :].astype(BF16)
    down[...] = acc[HALO : HALO + rows, :].astype(BF16)
    dright[...] = acc[HALO + rows :, :].astype(BF16)


def smem():
    return pl.BlockSpec(memory_space=pltpu.SMEM)


def vmem():
    return pl.BlockSpec(memory_space=pltpu.VMEM)


def attention_specs(rows, width, at):
    return [
        smem(),
        pl.BlockSpec((None, 1, rows), lambda j: (at(j), 0, 0)),
        pl.BlockSpec((None, 1, rows), lambda j: (at(j), 0, 0)),
        pl.BlockSpec((None, None, HALO, 2 * width), lambda j: (0, at(j), 0, 0)),
        pl.BlockSpec((rows, 3 * width), lambda j: (at(j), 0)),
        pl.BlockSpec((None, None, HALO, 2 * width), lambda j: (1, at(j), 0, 0)),
    ]


def attention_forward(ranges, low, high, halo_kv, qkv):
    micro, _, rows = low.shape
    width = qkv.shape[1] // 3
    window = rows + 2 * HALO
    at = lambda j: j
    return pl.pallas_call(
        forward_kernel,
        grid=(micro,),
        out_shape=(
            jax.ShapeDtypeStruct((micro * rows, width), BF16),
            jax.ShapeDtypeStruct((micro, 8, 2 * rows), F32),
        ),
        in_specs=attention_specs(rows, width, at),
        out_specs=(
            pl.BlockSpec((rows, width), lambda j: (j, 0)),
            pl.BlockSpec((None, 8, 2 * rows), lambda j: (j, 0, 0)),
        ),
        scratch_shapes=[pltpu.VMEM((window, 2 * width), BF16)],
        cost_estimate=pl.CostEstimate(
            flops=8 * rows * 640 * width * 4, bytes_accessed=16 * 1024 * 1024, transcendentals=0
        ),
        name="attn_fwd",
    )(ranges, low, high, halo_kv, qkv, halo_kv)


def attention_backward(m, ranges, low, high, halo_kv, qkv, log_sums, grad):
    rows, width = low.shape[2], grad.shape[1]
    window = rows + 2 * HALO
    at = lambda j: m
    return pl.pallas_call(
        partial(backward_kernel, m),
        grid=(1,),
        out_shape=(
            jax.ShapeDtypeStruct((rows, width), BF16),
            jax.ShapeDtypeStruct((HALO, 2 * width), BF16),
            jax.ShapeDtypeStruct((rows, 2 * width), BF16),
            jax.ShapeDtypeStruct((HALO, 2 * width), BF16),
        ),
        in_specs=attention_specs(rows, width, at)
        + [
            pl.BlockSpec((None, 8, 2 * rows), lambda j: (m, 0, 0)),
            pl.BlockSpec((rows, width), lambda j: (m, 0)),
        ],
        out_specs=(vmem(),) * 4,
        scratch_shapes=[
            pltpu.VMEM((window, 2 * width), BF16),
            pltpu.VMEM((window, 2 * width), F32),
        ],
        cost_estimate=pl.CostEstimate(
            flops=10 * rows * 640 * width * 4, bytes_accessed=16 * 1024 * 1024, transcendentals=0
        ),
        name="attn_bwd",
    )(ranges, low, high, halo_kv, qkv, halo_kv, log_sums, grad)


def column_sum(values):
    return jnp.sum(values, axis=0, keepdims=True)


def mlp_kernel(
    core,
    attended,
    tokens,
    cotangent,
    out_weight,
    vectors,
    up_weight,
    up_bias,
    down_weight,
    output,
    grad_mid,
    grad_attn,
    grad_attended,
    small,
    up_keep,
    up_send,
    down_keep,
    down_send,
    up_bias_grad,
    mid,
    normal,
    inv_std,
    branch,
    low,
    grad_mlp,
    acc,
    err,
):
    step = pl.program_id(0)
    out_bias, attn_scale = vectors[0:1, :], vectors[1:2, :]
    gain, shift = vectors[2:3, :], vectors[3:4, :]
    mlp_scale, down_bias = vectors[4:5, :], vectors[5:6, :]

    @pl.when(step == 0)
    def _():
        first = dot_nn(attended[...], out_weight[...]) + out_bias
        branch[...] = first
        total = tokens[...].astype(F32) + attn_scale * first
        mid[...] = total
        rows_n, inv = norm_stats(total)
        normal[...] = rows_n
        inv_std[...] = inv
        low[...] = (rows_n * gain + shift).astype(BF16)
        grad_mlp[...] = (mlp_scale * cotangent[...].astype(F32)).astype(BF16)
        acc[...] = jnp.zeros_like(acc)
        err[...] = jnp.zeros_like(err)

    up_pre = dot_nn(low[...], up_weight[...]) + up_bias[...]
    cdf = 0.5 * (1.0 + lax.erf(up_pre * 0.7071067811865476))
    slope = cdf + up_pre * (0.3989422804014327 * jnp.exp(-0.5 * up_pre * up_pre))
    active = (up_pre * cdf).astype(BF16)
    grad_up = (slope * dot_nt(grad_mlp[...], down_weight[...])).astype(BF16)
    acc[...] += dot_nn(active, down_weight[...])
    err[...] += dot_nt(grad_up, up_weight[...])
    up_bias_grad[0] = column_sum(grad_up.astype(F32))
    mine = core[0]
    up_grad = dot_tn(low[...], grad_up).astype(BF16)
    up_grad = up_grad.reshape(2, 2, up_keep.shape[2], up_keep.shape[3])
    up_keep[0] = jnp.where(mine == 0, up_grad[:, 0], up_grad[:, 1])
    up_send[0] = jnp.where(mine == 0, up_grad[:, 1], up_grad[:, 0])

    down_grad = dot_tn(grad_mlp[...], active).astype(BF16)
    down_grad = down_grad.reshape(down_keep.shape[0], down_keep.shape[3], down_keep.shape[4])

    @pl.when((step // 2) % 2 == mine)
    def _():
        down_keep[:, 0, 0] = down_grad

    @pl.when((step // 2) % 2 != mine)
    def _():
        down_send[:, 0, 0] = down_grad

    @pl.when(step == pl.num_programs(0) - 1)
    def _():
        grad_out = cotangent[...].astype(F32)
        mlp_branch = acc[...] + down_bias
        output[...] = (mid[...] + mlp_scale * mlp_branch).astype(BF16)
        e = err[...]
        rows_n = normal[...]
        scaled = e * gain
        mean_one = jnp.mean(scaled, axis=-1, keepdims=True)
        mean_two = jnp.mean(scaled * rows_n, axis=-1, keepdims=True)
        total = grad_out + inv_std[...] * (scaled - mean_one - rows_n * mean_two)
        grad_mid[...] = total
        low_grad = (attn_scale * total).astype(BF16)
        grad_attn[...] = low_grad
        grad_attended[...] = dot_nt(low_grad, out_weight[...]).astype(BF16)
        small[0:1, :] = column_sum(low_grad.astype(F32))
        small[1:2, :] = column_sum(total * branch[...])
        small[2:3, :] = column_sum(e * rows_n)
        small[3:4, :] = column_sum(e)
        small[4:5, :] = column_sum(grad_mlp[...].astype(F32))
        small[5:6, :] = column_sum(grad_out * mlp_branch)
        small[6:8, :] = jnp.zeros((2, small.shape[1]), F32)


def down_slot(step, mine):
    lead, at = 2 * (step // 4), step % 4
    low = lead + jnp.minimum(at, 1)
    high = jnp.where(at >= 2, lead + at - 2, jnp.maximum(lead - 1, 0))
    slot = jnp.where(mine == 0, low, high)
    return (0, slot // 2, slot % 2, 0, 0)


def mlp_call(core, attended, tokens, cotangent, out_weight, vectors, up_weight, up_bias, down_weight):
    rows, width = tokens.shape
    hidden = up_weight.shape[1]
    steps = hidden // FF_BLOCK
    cut = width // 8
    fixed = lambda shape: pl.BlockSpec(shape, lambda j, c: (0,) * len(shape))
    return pl.pallas_call(
        mlp_kernel,
        grid_spec=pltpu.PrefetchScalarGridSpec(
            num_scalar_prefetch=1,
            grid=(steps,),
            in_specs=[
                fixed((rows, width)),
                fixed((rows, width)),
                fixed((rows, width)),
                fixed((width, width)),
                fixed((8, width)),
                pl.BlockSpec((width, FF_BLOCK), lambda j, c: (0, j)),
                pl.BlockSpec((1, FF_BLOCK), lambda j, c: (0, j)),
                pl.BlockSpec((FF_BLOCK, width), lambda j, c: (j, 0)),
            ],
            out_specs=(
                fixed((rows, width)),
                fixed((rows, width)),
                fixed((rows, width)),
                fixed((rows, width)),
                fixed((8, width)),
                pl.BlockSpec((1, 2, width // 4, FF_BLOCK), lambda j, c: (j, 0, 0, 0)),
                pl.BlockSpec((1, 2, width // 4, FF_BLOCK), lambda j, c: (j, 0, 0, 0)),
                pl.BlockSpec((8, 1, 1, cut, FF_BLOCK), lambda j, c: down_slot(j, c[0])),
                pl.BlockSpec((8, 1, 1, cut, FF_BLOCK), lambda j, c: down_slot(j, 1 - c[0])),
                pl.BlockSpec((1, 1, FF_BLOCK), lambda j, c: (j // 2, 0, j % 2)),
            ),
            scratch_shapes=[
                pltpu.VMEM((rows, width), F32),
                pltpu.VMEM((rows, width), F32),
                pltpu.VMEM((rows, 1), F32),
                pltpu.VMEM((rows, width), F32),
                pltpu.VMEM((rows, width), BF16),
                pltpu.VMEM((rows, width), BF16),
                pltpu.VMEM((rows, width), F32),
                pltpu.VMEM((rows, width), F32),
            ],
        ),
        out_shape=(
            jax.ShapeDtypeStruct((rows, width), BF16),
            jax.ShapeDtypeStruct((rows, width), F32),
            jax.ShapeDtypeStruct((rows, width), BF16),
            jax.ShapeDtypeStruct((rows, width), BF16),
            jax.ShapeDtypeStruct((8, width), F32),
            jax.ShapeDtypeStruct((8, 2, width // 4, FF_BLOCK), BF16),
            jax.ShapeDtypeStruct((8, 2, width // 4, FF_BLOCK), BF16),
            jax.ShapeDtypeStruct((8, 2, 2, cut, FF_BLOCK), BF16),
            jax.ShapeDtypeStruct((8, 2, 2, cut, FF_BLOCK), BF16),
            jax.ShapeDtypeStruct((hidden // width, 1, width), F32),
        ),
        cost_estimate=pl.CostEstimate(
            flops=12 * rows * width * hidden, bytes_accessed=32 * 1024 * 1024, transcendentals=0
        ),
        name="mlp_both",
    )(core, attended, tokens, cotangent, out_weight, vectors, up_weight, up_bias, down_weight)


def grads_kernel(
    core, dq0, dq1, left0, left1, mid0, mid1, right0, right1, normed, halo, gattn, attended,
    one_keep, one_send, two_keep, two_send, sums, gall, xall, wt, og,
):
    rows, width = dq0.shape
    at = 0
    for m, (left, mid, right) in enumerate(((left0, mid0, right0), (left1, mid1, right1))):
        pieces = (
            (left[...], halo[0, m]),
            (mid[...], normed[m * rows : (m + 1) * rows]),
            (right[...], halo[1, m]),
        )
        for grad, low in pieces:
            gall[at : at + grad.shape[0], :] = grad
            xall[at : at + grad.shape[0], :] = low
            at += grad.shape[0]
    og[...] = dot_tn(gattn[...], attended[...])
    cols = 3 * width // 8
    cut = width // 8
    half = (cols + cut) // 2
    lane = lax.broadcasted_iota(jnp.int32, (half, 2 * (width // 4)), 1)
    first = lane < width // 4
    for k in range(2):
        if k == 0:
            wt[0:rows, :] = dot_tn(dq0[:, 0:rows], normed[0:rows, :]) + dot_tn(
                dq1[:, 0:rows], normed[rows:, :]
            )
            wt[rows:width, :] = dot_tn(dq0[:, rows:width], normed[0:rows, :]) + dot_tn(
                dq1[:, rows:width], normed[rows:, :]
            )
            wt[width:, :] = dot_tn(gall[:, 0 : 4 * cols - width], xall[...])
        else:
            wt[...] = dot_tn(gall[:, 4 * cols - width :], xall[...])
        for tt in range(4):
            t = 4 * k + tt
            for x in range(2):
                span = slice(2 * (width // 4) * x, 2 * (width // 4) * (x + 1))
                top = wt[cols * tt : cols * tt + half, span]
                bottom = jnp.concatenate(
                    [wt[cols * tt + half : cols * (tt + 1), span], og[cut * t : cut * (t + 1), span]],
                    axis=0,
                )
                even = jnp.where(first, top, pltpu.roll(bottom, width // 4, 1)).astype(BF16)
                odd = jnp.where(first, pltpu.roll(top, width // 4, 1), bottom).astype(BF16)
                keep = jnp.where(core[0] == 0, even, odd)
                send = jnp.where(core[0] == 0, odd, even)
                one_keep[t, x] = keep[: half // 2]
                two_keep[t, x] = keep[half // 2 :]
                one_send[t, x] = send[: half // 2]
                two_send[t, x] = send[half // 2 :]
    sums[0:1, :] = column_sum(dq0[...].astype(F32)) + column_sum(dq1[...].astype(F32))
    sums[1:2, :] = column_sum(gall[:, width:].astype(F32))
    sums[2:8, :] = jnp.zeros((6, width), F32)


def grads_call(*operands):
    _, width = operands[1].shape
    total = operands[9].shape[0]
    shape = (8, 2, width // 8, width // 2)
    window = total + 4 * HALO
    return pl.pallas_call(
        grads_kernel,
        in_specs=[smem()] + [vmem()] * 12,
        out_specs=(vmem(),) * 5,
        out_shape=(
            jax.ShapeDtypeStruct(shape, BF16),
            jax.ShapeDtypeStruct(shape, BF16),
            jax.ShapeDtypeStruct(shape, BF16),
            jax.ShapeDtypeStruct(shape, BF16),
            jax.ShapeDtypeStruct((8, width), F32),
        ),
        scratch_shapes=[
            pltpu.VMEM((window, 2 * width), BF16),
            pltpu.VMEM((window, width), BF16),
            pltpu.VMEM((3 * width // 2, width), F32),
            pltpu.VMEM((width, width), F32),
        ],
        cost_estimate=pl.CostEstimate(
            flops=12 * total * width * width, bytes_accessed=24 * 1024 * 1024, transcendentals=0
        ),
        name="qkv_grads",
    )(*operands)


def inner_kernel(
    dq0, dq1, mid0, mid1, fl0, fl1, fr0, fr1,
    weight, tokens, grad_mid, gain, small, up_bias_sum, qkv_sums, input_grad, vecs, acc,
):
    rows, width = dq0.shape
    vecs[0:6, :] = small[0:6, :]
    for k in range(4):
        vecs[6 + k : 7 + k, :] = up_bias_sum[k]
    vecs[12:16, :] = qkv_sums[0:4, :]
    sum_gain = jnp.zeros((1, width), F32)
    sum_shift = jnp.zeros((1, width), F32)
    for m, (dq, mid, left, right) in enumerate(((dq0, mid0, fl0, fr0), (dq1, mid1, fl1, fr1))):
        span = slice(m * rows, (m + 1) * rows)
        acc[...] = mid[...].astype(F32)
        acc[0:HALO, :] += left[...].astype(F32)
        acc[rows - HALO :, :] += right[...].astype(F32)
        f = dot_nt(dq[...], weight[:, 0:width]) + dot_nt(
            acc[...].astype(BF16), weight[:, width:]
        )
        rows_n, inv = norm_stats(tokens[span, :].astype(F32))
        scaled = f * gain[...]
        mean_one = jnp.mean(scaled, axis=-1, keepdims=True)
        mean_two = jnp.mean(scaled * rows_n, axis=-1, keepdims=True)
        input_grad[span, :] = grad_mid[span, :] + inv * (scaled - mean_one - rows_n * mean_two)
        sum_gain += column_sum(f * rows_n)
        sum_shift += column_sum(f)
    vecs[10:11, :] = sum_gain
    vecs[11:12, :] = sum_shift


def inner_call(*operands):
    rows, width = operands[0].shape
    total = operands[9].shape[0]
    return pl.pallas_call(
        inner_kernel,
        in_specs=[vmem()] * 15,
        out_specs=(vmem(), vmem()),
        out_shape=(
            jax.ShapeDtypeStruct((total, width), F32),
            jax.ShapeDtypeStruct((16, width), F32),
        ),
        scratch_shapes=[pltpu.VMEM((rows, 2 * width), F32)],
        cost_estimate=pl.CostEstimate(
            flops=6 * total * width * width, bytes_accessed=14 * 1024 * 1024, transcendentals=0
        ),
        name="inner",
    )(*operands)


def shift_right(values, size):
    return lax.ppermute(values, "head", [(i, i + 1) for i in range(size - 1)])


def shift_left(values, size):
    return lax.ppermute(values, "head", [(i + 1, i) for i in range(size - 1)])


def axis_bits(size):
    return size.bit_length() - 1


def bit_orders(tok_size, head_size):
    tok = [("tok", b) for b in range(axis_bits(tok_size))]
    head = [("head", b) for b in range(axis_bits(head_size))]
    turned = head[:1] + tok[1:2] + head[1:] + tok[:1] + tok[2:]
    return head + tok, head[:1] + tok + head[1:], turned


def swap_pairs(size, bit):
    return [(i, i ^ (1 << bit)) for i in range(size)]


class BlockSum:
    def __init__(self, keep, send, order, sizes):
        self.dims = [("tok", b) for b in reversed(range(axis_bits(sizes["tok"])))]
        self.dims += [("head", b) for b in reversed(range(axis_bits(sizes["head"])))]
        self.dims.remove(order[0])
        self.keep = keep.reshape((2,) * len(self.dims) + keep.shape[2:])
        self.first = send.reshape(self.keep.shape)
        self.order = list(order)
        self.sizes = sizes

    def cut(self):
        self.step = self.order.pop(0)
        if self.step not in self.dims:
            return [self.first]
        axis, bit = self.step
        where = self.dims.index(self.step)
        mine = (lax.axis_index(axis) >> bit) & 1
        send = lax.dynamic_index_in_dim(self.part, 1 - mine, where, keepdims=False)
        self.keep = lax.dynamic_index_in_dim(self.part, mine, where, keepdims=False)
        self.dims.pop(where)
        return [send]

    def send(self, parts):
        axis, bit = self.step
        return [lax.ppermute(parts[0], axis, swap_pairs(self.sizes[axis], bit))]

    def join(self, got):
        part = self.keep.astype(F32) + got[0].astype(F32)
        self.part = part.astype(BF16) if self.order else part


class SmallSum:
    def __init__(self, values, sizes):
        self.part = values
        self.sizes = sizes
        self.order = []
        for axis in ("head", "tok"):
            bits = axis_bits(sizes[axis])
            self.order += [(axis, b, min(2, bits - b)) for b in range(0, bits, 2)]

    def cut(self):
        self.step = self.order.pop(0)
        return [self.part]

    def send(self, parts):
        axis, bit, count = self.step
        size = self.sizes[axis]
        masks = [1 << bit] if count == 1 else [1 << bit, 2 << bit, 3 << bit]
        return [lax.ppermute(parts[0], axis, [(i, i ^ m) for i in range(size)]) for m in masks]

    def join(self, got):
        part = self.part + got[0]
        self.part = part + (got[1] + got[2]) if len(got) > 1 else part


def launch(sums, *tied):
    pieces = [s.cut() for s in sums]
    flat, tied = lax.optimization_barrier((pieces, tied))
    flights = []
    for s, p in zip(sums, flat):
        flights.append(s.send(p))
    return flights, tied


def land(sums, flights, *tied):
    flights, tied = lax.optimization_barrier((flights, tied))
    for s, got in zip(sums, flights):
        s.join(got)
    return tied


def regroup_up(blocks, more):
    lead, head, rows, cols = blocks.shape
    blocks = blocks.reshape(lead, head, rows, more, cols // more).transpose(0, 3, 1, 2, 4)
    return blocks.reshape(lead * more, head, rows, cols // more)


def regroup_down(blocks, more):
    lead, head, half, rows, cols = blocks.shape
    blocks = blocks.reshape(lead, head, half, more, rows // more, cols)
    return blocks.transpose(0, 3, 1, 2, 4, 5).reshape(lead * more, head, half, rows // more, cols)


def regroup_qkv(one, two, more):
    tall = jnp.concatenate([one, two], axis=2)
    tall = jnp.concatenate(jnp.split(tall, 2, axis=3), axis=2)
    lead, head, rows, cols = tall.shape
    cut = 3 * rows // 4
    pieces = [tall[:, :, :cut], tall[:, :, cut:]]
    pieces = [p.reshape(lead, head, more, -1, cols).transpose(0, 2, 1, 3, 4) for p in pieces]
    tall = jnp.concatenate(pieces, axis=3).reshape(lead * more, head, rows // more, cols)
    return tuple(jnp.split(tall, 2, axis=2))


def per_device(
    sizes,
    tokens,
    crop_start,
    crop_len,
    attn_gain,
    attn_shift,
    qkv_weight,
    query_bias,
    value_bias,
    out_weight,
    out_bias,
    attn_scale,
    mlp_gain,
    mlp_shift,
    up_weight,
    up_bias,
    down_weight,
    down_bias,
    mlp_scale,
    cotangent,
):
    micro, rows, width = tokens.shape
    hidden = up_weight.shape[1]
    tok_size, head_size = sizes["tok"], sizes["head"]
    window = rows + 2 * HALO
    head_at = lax.axis_index("head")
    order_a, order_b, order_c = bit_orders(tok_size, head_size)
    kv_bias = jnp.concatenate([jnp.zeros_like(value_bias), value_bias])
    qkv_bias = jnp.concatenate([query_bias, kv_bias])

    halo_left = shift_right(tokens[:, rows - HALO :, :], head_size)
    halo_right = shift_left(tokens[:, :HALO, :], head_size)

    total_rows = micro * rows
    inputs_f = tokens.reshape(total_rows, width).astype(F32)
    normal_one, _ = norm_stats(inputs_f)
    normed_low = (normal_one * attn_gain + attn_shift).astype(BF16)
    qkv = (dot_nn(normed_low, qkv_weight) + qkv_bias).astype(BF16)

    halo = jnp.stack([halo_left, halo_right]).reshape(2 * micro * HALO, width)
    halo_normal, _ = norm_stats(halo.astype(F32))
    halo_low = (halo_normal * attn_gain + attn_shift).astype(BF16)
    halo_kv = (dot_nn(halo_low, qkv_weight[:, width:]) + kv_bias).astype(BF16)
    halo_kv = halo_kv.reshape(2, micro, HALO, 2 * width)

    ranges, lows, highs = [], [], []
    for m in range(micro):
        low, high = crop_bounds(
            crop_start[m, 0], crop_len[m, 0], head_at * rows, rows, head_size * rows
        )
        ranges.append(tile_ranges(low, high, window))
        lows.append(low[None, :])
        highs.append(high[None, :])
    crops = (jnp.stack(ranges), jnp.stack(lows), jnp.stack(highs), halo_kv, qkv)
    attended, log_sums = attention_forward(*crops)

    vectors = jnp.stack(
        [
            out_bias,
            attn_scale,
            mlp_gain,
            mlp_shift,
            mlp_scale,
            down_bias,
            jnp.zeros_like(out_bias),
            jnp.zeros_like(out_bias),
        ]
    )
    core = (head_at & 1).astype(jnp.int32).reshape(1)
    (
        output,
        grad_mid,
        grad_attn,
        grad_attended,
        small,
        up_keep,
        up_send,
        down_keep,
        down_send,
        up_bias_sum,
    ) = mlp_call(
        core,
        attended,
        tokens.reshape(total_rows, width),
        cotangent.reshape(total_rows, width),
        out_weight,
        vectors,
        up_weight,
        up_bias[None, :],
        down_weight,
    )
    more = tok_size // 8
    if more > 1:
        up_keep, up_send = regroup_up(up_keep, more), regroup_up(up_send, more)
        down_keep, down_send = regroup_down(down_keep, more), regroup_down(down_send, more)
    up_sum = BlockSum(up_keep, up_send, order_b, sizes)
    down_sum = BlockSum(down_keep, down_send, order_c, sizes)

    grads = []
    early = [up_sum, down_sum]
    for m in range(micro):
        flights, (grad_attended,) = launch(early, grad_attended)
        dq, dleft, dmid, dright = attention_backward(m, *crops, log_sums, grad_attended)
        from_left = shift_right(dright, head_size)
        from_right = shift_left(dleft, head_size)
        (dq,) = land(early, flights, dq)
        grads.append((dq, dleft, dmid, dright, from_left, from_right))
    (dq0, l0, m0, r0, fl0, fr0), (dq1, l1, m1, r1, fl1, fr1) = grads
    flights, (dq1,) = launch(early, dq1)
    halo_low = halo_low.reshape(2, micro, HALO, width)
    one_keep, one_send, two_keep, two_send, qkv_sums = grads_call(
        core, dq0, dq1, l0, l1, m0, m1, r0, r1, normed_low, halo_low, grad_attn, attended
    )
    if more > 1:
        one_keep, two_keep = regroup_qkv(one_keep, two_keep, more)
        one_send, two_send = regroup_qkv(one_send, two_send, more)
    late = [
        BlockSum(one_keep, one_send, order_a, sizes),
        BlockSum(two_keep, two_send, order_b, sizes),
    ]
    late_flights, _ = launch(late)
    land(early, flights)
    flights, _ = launch(early)
    land(late, late_flights)
    late_flights, (dq0,) = launch(late, dq0)
    land(early, flights)
    flights, _ = launch(early)
    input_grad, vecs = inner_call(
        dq0,
        dq1,
        m0,
        m1,
        fl0,
        fl1,
        fr0,
        fr1,
        qkv_weight,
        tokens.reshape(total_rows, width),
        grad_mid,
        attn_gain[None, :],
        small,
        up_bias_sum,
        qkv_sums,
    )
    (vecs,) = land(late, late_flights, vecs)
    land(early, flights)
    vecs = SmallSum(vecs, sizes)
    everything = late + early + [vecs]
    while any(s.order for s in everything):
        active = [s for s in everything if s.order]
        flights, _ = launch(active)
        land(active, flights)
    one, two, up, down = [s.part for s in late + early]
    vecs = vecs.part
    tall = jnp.concatenate([one, two], axis=0)
    if more == 1:
        tall = jnp.concatenate(jnp.split(tall, 2, axis=1), axis=0)
    grad_qkv = tall[: 3 * width // tok_size].T
    grad_out = tall[3 * width // tok_size :].T
    grad_up_weight = up
    grad_down = down.transpose(0, 2, 1).reshape(hidden // head_size, width // tok_size)
    early = vecs[:6]
    late = vecs[10:14]
    return (
        output.reshape(micro, rows, width),
        input_grad.reshape(micro, rows, width),
        late[0],
        late[1],
        grad_qkv,
        late[2],
        late[3],
        grad_out,
        early[0],
        early[1],
        early[2],
        early[3],
        grad_up_weight,
        vecs[6:10].reshape(hidden),
        grad_down,
        early[4],
        early[5],
    )


def solution(mesh):
    sizes = {"tok": mesh.shape["tok"], "head": mesh.shape["head"]}
    rows = P(None, ("tok", "head"), None)
    crops = P(None, "tok", None)
    whole = P()
    split = P("head", "tok")

    def body(*args):
        return per_device(sizes, *args)

    return jax.shard_map(
        body,
        mesh=mesh,
        in_specs=(rows, crops, crops) + (whole,) * 15 + (rows,),
        out_specs=(
            rows,
            rows,
            whole,
            whole,
            split,
            whole,
            whole,
            split,
            whole,
            whole,
            whole,
            whole,
            split,
            whole,
            split,
            whole,
            whole,
        ),
        check_vma=False,
    )
```
